32 devices in a mesh: groups: 2 (over y), ctx: 4 (over z), fsdp: 2 (over x), sub: 2 (over core).
Axes of the slice: x: 2, y: 2, z: 4, core: 2. Of those that a mesh axis runs over, the one named last changes fastest.
Arguments:
- streams: bfloat16 [3, 2048, 4096], P(None, ('groups', 'ctx', 'sub'), 'fsdp'), parts along dimension 1, may hold values from -6 to 6
- feat_taps: float32 [3, 7, 4096], P(None, None, 'fsdp'), may hold values from -2.4 to 2.4
- long_filter: bfloat16 [128, 4096], P('ctx', 'fsdp'), may hold values from -0.5 to 0.5
- upstream: bfloat16 [2048, 4096], P(('groups', 'ctx', 'sub'), 'fsdp'), parts along dimension 0, may hold values from -6 to 6
- score_dir: float32 [4096], P('fsdp'), may hold values from -21 to 21
- seg_lengths: int32 [16], P('groups'), parts along dimension 0, may hold values from 1 to 512, 1024 in all
- list_ids: int32 [16], P('groups'), parts along dimension 0, may hold values from 0 to 1
Outputs:
- d_streams: bfloat16 [3, 2048, 4096], P(None, ('groups', 'ctx', 'sub'), 'fsdp'), parts along dimension 1
- d_feat: float32 [6, 7, 4096], P('groups', None, 'fsdp'), parts along dimension 0
- d_filter: float32 [256, 4096], P(('groups', 'ctx'), 'fsdp'), parts along dimension 0
The draws below stay inside these ranges and needn't reach their ends.
There are 2 independent parts, one for each index of `groups`. The reference program is written for one: setup_inputs(seed, part) draws one part's arguments, and reference() takes and returns one part's arrays. A program takes and returns all parts, laid end to end along the dimension named above; an argument that names none is the same for every part. Nothing has to cross between parts.
Inputs may be any that keep to these rules, and one draw needn't show every extreme that they name: `seg_lengths`: the lengths sum to 1024 and the longest segment has exactly 512 tokens.
All inputs are finite; a program needn't handle non-finite values.
Results may differ from the reference program's by a relative error of at most 0.012.
Values may be sent and summed in bfloat16 or wider, within the bound.
A program may use at most 64 MiB of HBM per device.

```python
import math
import jax
import jax.numpy as jnp
import numpy as np
from jax import lax

C = 4096
LH = 128
KF = 7
TOKENS = 1024
SEGS = 8
MOST = 512
LISTS = 2


def with_ends(array, stream_key, smallest, top_value):
    extent = array.shape
    spot = [jax.random.randint(jax.random.fold_in(stream_key, axis), (), 0, extent[axis]) for axis in range(len(extent))]
    array = array.at[tuple(spot)].set(smallest)
    longest = extent.index(max(extent))
    spot[longest] = (spot[longest] + 1) % extent[longest]
    return array.at[tuple(spot)].set(top_value)


def steps_of(key, shape, pieces, smallest, top_value):
    level, own = 1.0, jax.random.fold_in(key, 6)
    for axis_at, blocks in pieces:
        steps = jnp.exp(jax.random.uniform(jax.random.fold_in(own, axis_at), (blocks,), jnp.float32, smallest / len(pieces), top_value / len(pieces)))
        level = level * jnp.repeat(steps, shape[axis_at] // blocks).reshape([-1 if axis == axis_at else 1 for axis in range(len(shape))])
    return level


def profile(count, total, limit, skew):
    portions = [(1 << 20) // math.isqrt(rank ** skew) + 1 for rank in range(2, count + 1)]
    spare, given = total - limit - (count - 1), [1] * (count - 1)
    while spare > 0:
        free = [i for i in range(count - 1) if given[i] < limit]
        pool, budget = sum([portions[i] for i in free]), spare
        for i in free:
            addition = min(limit - given[i], max(1, budget * portions[i] // pool), spare)
            given[i] = given[i] + addition
            spare = spare - addition
    return np.array([limit] + given)


def uneven_parts(own_key, amount, total, reach, lean):
    if amount == 2:
        one = jax.random.randint(own_key, (), max(1, total - reach), min(reach, total - 1) + 1)
        return jnp.stack([one, total - one])
    sizes = jnp.asarray(profile(amount, total, reach, lean), jnp.int32)
    pairs = (amount - 1) // 2
    source_of, taker = sizes[1:1 + 2 * pairs:2], sizes[2:2 + 2 * pairs:2]
    margin = jnp.minimum(source_of - 1, reach - taker)
    shifted = jax.random.randint(jax.random.fold_in(own_key, 1), (pairs,), 0, 1 << 20) % (margin + 1)
    sizes = sizes.at[1:1 + 2 * pairs:2].set(source_of - shifted).at[2:2 + 2 * pairs:2].set(taker + shifted)
    return sizes[jax.random.permutation(jax.random.fold_in(own_key, 2), amount)]


def gaussian(own_key, shape, spread, bound, shards=(), kind=jnp.bfloat16):
    values = jax.random.normal(own_key, shape, jnp.float32) * spread
    if len(shards) > 0:
        values = steps_of(own_key, shape, shards, -0.22, 0.18) * values
    return jnp.clip(values, min=-bound, max=bound).astype(kind)


def setup_inputs(seed: int = 0, part: int = 0) -> dict:
    keys = jax.random.split(jax.random.key(seed), 8)
    own_keys = jax.random.split(jax.random.fold_in(keys[7], part), 8)
    return {
        "streams": gaussian(own_keys[0], (3, TOKENS, C), 1.0, 6.0, ((1, 8), (2, 2))),
        "feat_taps": gaussian(keys[1], (3, KF, C), 0.4, 2.4, ((2, 2),), jnp.float32),
        "long_filter": gaussian(keys[2], (LH, C), LH ** -0.5, 0.5, ((0, 4), (1, 2))),
        "upstream": gaussian(own_keys[3], (TOKENS, C), 1.0, 6.0, ((0, 8), (1, 2))),
        "score_dir": gaussian(keys[4], (C,), 3.5, 21.0, ((0, 2),), jnp.float32),
        "seg_lengths": uneven_parts(own_keys[5], SEGS, TOKENS, MOST, 2).astype(jnp.int32),
        "list_ids": with_ends(jax.random.randint(own_keys[6], (SEGS,), 0, LISTS), jax.random.fold_in(own_keys[6], 1), 0, LISTS - 1).astype(jnp.int32),
    }


HIGH = lax.Precision.HIGHEST


def tap_block(tap_count):
    return 16 if tap_count % 16 == 0 else tap_count


def segment_age(seg_lengths, positions):
    offsets = jnp.cumsum(seg_lengths, dtype=jnp.int32) - seg_lengths
    member = offsets[None, :] <= positions[:, None]
    seg_index = jnp.sum(member.astype(jnp.int32), axis=1, dtype=jnp.int32) - 1
    seg_start = jnp.max(jnp.where(member, offsets[None, :], 0), axis=1)
    return seg_index, (positions - seg_start).astype(jnp.int32)


def causal_taps(tap_table, extended, row_age, tok_rows):
    tap_count = tap_table.shape[0]
    per_turn = tap_block(tap_count)

    def advance(b, running):
        for m in range(per_turn):
            j = b * per_turn + m
            window = lax.dynamic_slice_in_dim(extended, tap_count - 1 - j, tok_rows, 0)
            weight_row = lax.dynamic_index_in_dim(tap_table, j, 0, keepdims=False)
            running = running + jnp.where((row_age >= j)[:, None], weight_row[None, :] * window.astype(jnp.float32), 0.0)
        return running

    start_sum = jnp.zeros((tok_rows, extended.shape[1]), jnp.float32)
    return lax.fori_loop(0, tap_count // per_turn, advance, start_sum)


def reverse_taps(tap_table, extended, ext_age, tok_rows):
    tap_count = tap_table.shape[0]
    per_turn = tap_block(tap_count)

    def advance(b, running):
        for m in range(per_turn):
            j = b * per_turn + m
            window = lax.dynamic_slice_in_dim(extended, j, tok_rows, 0)
            keep = lax.dynamic_slice_in_dim(ext_age, j, tok_rows, 0) >= j
            weight_row = lax.dynamic_index_in_dim(tap_table, j, 0, keepdims=False)
            running = running + jnp.where(keep[:, None], weight_row[None, :] * window.astype(jnp.float32), 0.0)
        return running

    start_sum = jnp.zeros((tok_rows, extended.shape[1]), jnp.float32)
    return lax.fori_loop(0, tap_count // per_turn, advance, start_sum)


def correlate_taps(gradient, extended, row_age, tap_count, tok_rows):
    per_turn = tap_block(tap_count)

    def advance(b, result):
        collected = []
        for m in range(per_turn):
            j = b * per_turn + m
            window = lax.dynamic_slice_in_dim(extended, tap_count - 1 - j, tok_rows, 0)
            product = gradient.astype(jnp.float32) * window.astype(jnp.float32)
            collected.append(jnp.sum(jnp.where((row_age >= j)[:, None], product, 0.0), axis=0))
        return lax.dynamic_update_slice_in_dim(result, jnp.stack(collected), b * per_turn, 0)

    start_rows = jnp.zeros((tap_count, gradient.shape[1]), jnp.float32)
    return lax.fori_loop(0, tap_count // per_turn, advance, start_rows)


def list_coef(totals, seg_lengths, list_ids):
    length_f = seg_lengths.astype(jnp.float32)
    scores = totals / length_f
    mates = (list_ids[:, None] == list_ids[None, :]).astype(jnp.float32)
    mean_score = jnp.dot(mates, scores, precision=HIGH) / jnp.sum(mates, axis=1)
    return (scores - mean_score) / length_f


def reference(streams, feat_taps, long_filter, upstream, score_dir, seg_lengths, list_ids):
    tok_rows = streams.shape[1]
    positions = jnp.arange(tok_rows, dtype=jnp.int32)
    seg_index, row_age = segment_age(seg_lengths, positions)
    age_span = jnp.concatenate([row_age, jnp.zeros((LH - 1,), jnp.int32)])
    front = [jnp.pad(streams[i], ((KF - 1, 0), (0, 0))) for i in range(3)]
    featured = [causal_taps(feat_taps[i], front[i], row_age, tok_rows).astype(jnp.bfloat16) for i in range(3)]
    query, key_feat, value_feat = featured
    product = (key_feat.astype(jnp.float32) * value_feat.astype(jnp.float32)).astype(jnp.bfloat16)
    filt = long_filter.astype(jnp.float32)
    prod_ext = jnp.pad(product, ((LH - 1, 0), (0, 0)))
    mixed = causal_taps(filt, prod_ext, row_age, tok_rows)
    out_y = query.astype(jnp.float32) * mixed
    projected = jnp.dot(out_y, score_dir, precision=HIGH)
    onehot = (seg_index[:, None] == jnp.arange(SEGS, dtype=jnp.int32)[None, :]).astype(jnp.float32)
    totals = jnp.dot(projected, onehot, precision=HIGH)
    coef = list_coef(totals, seg_lengths, list_ids)
    tok_coef = jnp.dot(onehot, coef, precision=HIGH)
    d_out = upstream.astype(jnp.float32) + tok_coef[:, None] * score_dir[None, :]
    d_query = (d_out * mixed).astype(jnp.bfloat16)
    d_mixed = (d_out * query.astype(jnp.float32)).astype(jnp.bfloat16)
    dm_ext = jnp.pad(d_mixed, ((0, LH - 1), (0, 0)))
    d_prod = reverse_taps(filt, dm_ext, age_span, tok_rows)
    d_key = (d_prod * value_feat.astype(jnp.float32)).astype(jnp.bfloat16)
    d_value = (d_prod * key_feat.astype(jnp.float32)).astype(jnp.bfloat16)
    d_filter = correlate_taps(d_mixed, prod_ext, row_age, LH, tok_rows)
    grads = [d_query, d_key, d_value]
    d_streams = []
    d_feat = []
    for i in range(3):
        grad_ext = jnp.pad(grads[i], ((0, KF - 1), (0, 0)))
        d_streams.append(reverse_taps(feat_taps[i], grad_ext, age_span, tok_rows).astype(jnp.bfloat16))
        d_feat.append(correlate_taps(grads[i], front[i], row_age, KF, tok_rows))
    return jnp.stack(d_streams), jnp.stack(d_feat), d_filter
```

```python
import functools

import jax
import jax.numpy as jnp
import numpy as np
from jax import lax
from jax.experimental import pallas as pl
from jax.experimental.pallas import tpu as pltpu
from jax.sharding import PartitionSpec as P

LH = 128
KF = 7
N2 = 2 * LH
F32 = jnp.float32
BF16 = jnp.bfloat16

_K, _N = np.meshgrid(np.arange(LH), np.arange(N2), indexing="ij")
_ANGLE = np.pi * (2 * _K + 1) * _N / N2
FWD = np.concatenate([np.cos(_ANGLE), -np.sin(_ANGLE)], axis=0).astype(np.float32)
INV = (FWD.T / LH).astype(np.float32)


def passed_along(value, axis, steps):
    count = lax.axis_size(axis)
    leading, last = (max(0, -steps), min(count, count - steps))
    return lax.ppermute(value, axis, [(source, source + steps) for source in range(leading, last)])


def rotated(value, axis, steps):
    count = lax.axis_size(axis)
    return lax.ppermute(value, axis, [(i, (i + steps) % count) for i in range(count)])


def segments_at(seg_lengths, positions):
    offsets = jnp.cumsum(seg_lengths, dtype=jnp.int32) - seg_lengths
    member = offsets[None, :] <= positions[:, None]
    seg_index = jnp.sum(member.astype(jnp.int32), axis=1, dtype=jnp.int32) - 1
    seg_start = jnp.max(jnp.where(member, offsets[None, :], 0), axis=1)
    return (seg_index, positions - seg_start)


def dot(a, b):
    return jnp.dot(a, b, preferred_element_type=F32)


def feat_kernel(shift_ref, x_ref, halo_ref, taps_ref, feat_ref, z_ref, ext_ref):
    rows = x_ref.shape[1]
    feats = []
    for i in range(3):
        ext_ref[0:16, :] = halo_ref[i]
        ext_ref[16:, :] = x_ref[i]
        ext = ext_ref[...]
        total = jnp.zeros((rows, x_ref.shape[2]), F32)
        for j in range(KF):
            total = total + taps_ref[i, j : j + 1, :] * dot(
                shift_ref[j * rows : (j + 1) * rows, :], ext
            )
        feats.append(total.astype(BF16))
        feat_ref[i] = feats[i]
    z_ref[...] = (feats[1].astype(F32) * feats[2].astype(F32)).astype(BF16)


def mix_kernel(
    span_ref, fwd_ref, inv_ref, fil_fwd_ref, colseg_ref, rowseg_ref, prev_ref, z_ref, fil_ref,
    q_ref, dir_ref, w_ref, proj_ref, ext_ref,
):
    rows = z_ref.shape[0]
    ext_ref[0:rows, :] = prev_ref[...]
    ext_ref[rows:, :] = z_ref[...]
    spec = dot(fil_fwd_ref[...], fil_ref[...])
    f_re, f_im = spec[:LH], spec[LH:]
    w_ref[...] = jnp.zeros(w_ref.shape, F32)

    def one(s, carry):
        fwd = jnp.where(colseg_ref[...] == s, fwd_ref[...], 0.0).astype(BF16)
        hat = dot(fwd, ext_ref[...])
        z_re, z_im = hat[:LH], hat[LH:]
        prod = jnp.concatenate(
            [(f_re * z_re - f_im * z_im).astype(BF16), (f_re * z_im + f_im * z_re).astype(BF16)],
            axis=0,
        )
        inv = jnp.where(rowseg_ref[...] == s, inv_ref[...], 0.0).astype(BF16)
        w_ref[...] += dot(inv, prod)
        return carry

    lax.fori_loop(span_ref[0], span_ref[1] + 1, one, 0)
    weighted = q_ref[0].astype(F32) * w_ref[...] * dir_ref[...]
    part = weighted[:, 0:128]
    for b in range(1, weighted.shape[1] // 128):
        part = part + weighted[:, b * 128 : (b + 1) * 128]

    @pl.when(pl.program_id(0) == 0)
    def _():
        proj_ref[...] = jnp.zeros(proj_ref.shape, F32)

    proj_ref[...] += part


def grad_kernel(
    span_ref, fwd_ref, inv_ref, fil_fwd_ref, colseg_ref, rowseg_ref, tokcoef_ref, up_ref,
    up_next_ref, q_next_ref, dir_ref, feat_ref, w_ref, z_ref, fil_ref,
    da_ref, dfil_ref, ext_ref, dz_ref, corr_ref,
):
    rows = z_ref.shape[0]
    d_out = up_ref[...].astype(F32) + tokcoef_ref[0:rows, :] * dir_ref[...]
    da_ref[0] = (d_out * w_ref[...]).astype(BF16)
    ext_ref[0:rows, :] = (d_out * feat_ref[0].astype(F32)).astype(BF16)
    d_next = up_next_ref[...].astype(F32) + tokcoef_ref[rows:, :] * dir_ref[...]
    ext_ref[rows:, :] = (d_next * q_next_ref[...].astype(F32)).astype(BF16)
    spec = dot(fil_fwd_ref[...], fil_ref[...])
    f_re, f_im = spec[:LH], spec[LH:]
    dz_ref[...] = jnp.zeros(dz_ref.shape, F32)
    corr_ref[...] = jnp.zeros(corr_ref.shape, F32)

    def one(s, carry):
        fwd = jnp.where(colseg_ref[...] == s, fwd_ref[...], 0.0).astype(BF16)
        hat = dot(fwd, ext_ref[...])
        d_re, d_im = hat[:LH], hat[LH:]
        prod = jnp.concatenate(
            [(f_re * d_re + f_im * d_im).astype(BF16), (f_re * d_im - f_im * d_re).astype(BF16)],
            axis=0,
        )
        inv = jnp.where(rowseg_ref[...] == s, inv_ref[...], 0.0).astype(BF16)
        dz_ref[...] += dot(inv, prod)
        zhat = dot(fwd[:, :rows], z_ref[...])
        z_re, z_im = zhat[:LH], zhat[LH:]
        corr_ref[:LH] += z_re * d_re + z_im * d_im
        corr_ref[LH:] += z_re * d_im - z_im * d_re
        return carry

    lax.fori_loop(span_ref[0], span_ref[1] + 1, one, 0)
    d_prod = dz_ref[...]
    da_ref[1] = (d_prod * feat_ref[2].astype(F32)).astype(BF16)
    da_ref[2] = (d_prod * feat_ref[1].astype(F32)).astype(BF16)
    dfil_ref[...] = dot(inv_ref[...].astype(BF16), corr_ref[...].astype(BF16)).astype(BF16)


def back_kernel(shift_ref, da_ref, halo_ref, x_ref, taps_ref, dx_ref, dtaps_ref, ext_ref):
    rows = x_ref.shape[1]
    for i in range(3):
        ext_ref[0:rows, :] = da_ref[i]
        ext_ref[rows:, :] = halo_ref[i]
        ext = ext_ref[...]
        own = x_ref[i].astype(F32)
        total = jnp.zeros((rows, x_ref.shape[2]), F32)
        for j in range(KF):
            moved = dot(shift_ref[j * rows : (j + 1) * rows, :], ext)
            total = total + taps_ref[i, j : j + 1, :] * moved
            dtaps_ref[8 * i + j : 8 * i + j + 1, :] = jnp.sum(own * moved, axis=0, keepdims=True)
        dtaps_ref[8 * i + 7 : 8 * i + 8, :] = jnp.zeros((1, x_ref.shape[2]), F32)
        dx_ref[i] = total.astype(BF16)


def const_spec(shape):
    return pl.BlockSpec(shape, lambda b, *_: (0,) * len(shape))


def rows_spec(rows, width):
    return pl.BlockSpec((rows, width), lambda b, *_: (0, b))


def stack_spec(count, rows, width):
    return pl.BlockSpec((count, rows, width), lambda b, *_: (0, 0, b))


def list_coef(totals, seg_lengths, list_ids):
    length_f = seg_lengths.astype(F32)
    scores = totals / length_f
    mates = (list_ids[:, None] == list_ids[None, :]).astype(F32)
    mean_score = jnp.sum(mates * scores[None, :], axis=1) / jnp.sum(mates, axis=1)
    return (scores - mean_score) / length_f


def total_kernel(sizes, part_ref, out_ref, slots, send_sem, recv_sem):
    n_ctx, n_fsdp, n_sub = sizes
    count = n_ctx * n_fsdp * n_sub
    me = (lax.axis_index("ctx") * n_fsdp + lax.axis_index("fsdp")) * n_sub + lax.axis_index("sub")
    group = lax.axis_index("groups")

    def where(r):
        peer = lax.rem(me + r, count)
        return (
            group,
            peer // (n_fsdp * n_sub),
            lax.rem(peer // n_sub, n_fsdp),
            lax.rem(peer, n_sub),
        )

    barrier = pltpu.get_barrier_semaphore()

    def greet(r, carry):
        pl.semaphore_signal(
            barrier, inc=1, device_id=where(r), device_id_type=pl.DeviceIdType.MESH
        )
        return carry

    lax.fori_loop(1, count, greet, 0)
    pl.semaphore_wait(barrier, count - 1)

    def copy(r):
        return pltpu.make_async_remote_copy(
            src_ref=part_ref,
            dst_ref=slots.at[r],
            send_sem=send_sem.at[r],
            recv_sem=recv_sem.at[r],
            device_id=where(r),
            device_id_type=pl.DeviceIdType.MESH,
        )

    def begin(r, carry):
        copy(r).start()
        return carry

    def end(r, carry):
        copy(r).wait()
        return carry

    lax.fori_loop(1, count, begin, 0)
    lax.fori_loop(1, count, end, 0)
    slots[0] = part_ref[...]

    def add(i, total):
        return total + slots[lax.rem(me - i + count, count)]

    out_ref[...] = lax.fori_loop(0, count, add, jnp.zeros(out_ref.shape, F32))


def group_total(part, sizes):
    count = sizes[0] * sizes[1] * sizes[2]
    return pl.pallas_call(
        functools.partial(total_kernel, sizes),
        out_shape=jax.ShapeDtypeStruct(part.shape, F32),
        in_specs=[pl.BlockSpec(memory_space=pltpu.VMEM)],
        out_specs=pl.BlockSpec(memory_space=pltpu.VMEM),
        scratch_shapes=[
            pltpu.VMEM((count,) + part.shape, F32),
            pltpu.SemaphoreType.DMA((count,)),
            pltpu.SemaphoreType.DMA((count,)),
        ],
        compiler_params=pltpu.CompilerParams(collective_id=0, has_side_effects=True),
        name="group_total",
    )(part)


def gathered_filter(shard):
    count = lax.axis_size("ctx")
    ctx, sub = lax.axis_index("ctx"), lax.axis_index("sub")
    rows = shard.shape[0]
    half = rows // 2
    mine = lax.dynamic_slice_in_dim(shard, sub * half, half, 0)
    parts = [mine] + [rotated(mine, "ctx", r) for r in range(1, count)]
    own = jnp.concatenate(parts, axis=0)
    other = rotated(own, "sub", 1)
    place = jnp.arange(LH, dtype=jnp.int32)
    turn = (place // half) % count
    side = place // (half * count)
    held = (ctx - turn + count) % count
    which = jnp.where(side == 0, sub, 1 - sub)
    return jnp.concatenate([own, other], axis=0), held * rows + which * half + place % half


def reduced(filter_part, taps_part, shard_rows):
    count = lax.axis_size("ctx")
    ctx, sub = lax.axis_index("ctx"), lax.axis_index("sub")
    both = jnp.concatenate([filter_part, taps_part.astype(BF16)], axis=0)
    width = both.shape[1] // 2
    given = lax.dynamic_slice_in_dim(both, (1 - sub) * width, width, 1)
    kept = lax.dynamic_slice_in_dim(both, sub * width, width, 1)
    chip = kept.astype(F32) + rotated(given, "sub", 1).astype(F32)
    sent = chip.astype(BF16)
    total = jnp.concatenate(
        [lax.dynamic_slice_in_dim(chip, ctx * shard_rows, shard_rows, 0), chip[LH:]], axis=0
    )
    for r in range(1, count):
        piece = jnp.concatenate(
            [
                lax.dynamic_slice_in_dim(sent, ((ctx + r) % count) * shard_rows, shard_rows, 0),
                sent[LH:],
            ],
            axis=0,
        )
        total = total + rotated(piece, "ctx", r).astype(F32)
    other = rotated(total, "sub", 1)
    return jnp.where(
        sub == 0,
        jnp.concatenate([total, other], axis=1),
        jnp.concatenate([other, total], axis=1),
    )


def local(sizes, streams, feat_taps, long_filter, upstream, score_dir, seg_lengths, list_ids):
    rows, chans = streams.shape[1:]
    seg_count = seg_lengths.shape[0]
    width = min(512, chans)
    grid = (chans // width,)
    line = ("ctx", "sub")

    stream_rim = passed_along(streams[:, rows - 16 :, :], line, 1)
    up_next = passed_along(upstream, line, -1)
    filt, tap_of = gathered_filter(long_filter)

    first_row = lax.axis_index(line) * rows
    positions = first_row - rows + jnp.arange(3 * rows, dtype=jnp.int32)
    seg_span, age_span = segments_at(seg_lengths, positions)
    age_now = age_span[rows : 2 * rows]
    age_on = age_span[rows:]
    seg_now = seg_span[rows : 2 * rows]
    limits = jnp.stack([seg_now[0], seg_now[rows - 1]])
    taps = jnp.arange(KF, dtype=jnp.int32)[:, None, None]
    at = jnp.arange(rows, dtype=jnp.int32)[None, :, None]
    spot = jnp.arange(rows + 16, dtype=jnp.int32)[None, None, :]
    shift = ((spot == 16 + at - taps) & (taps <= age_now[None, :, None])).astype(BF16)
    shift = shift.reshape(KF * rows, rows + 16)
    unshift = ((spot == at + taps) & (taps <= age_on[None, None, : rows + 16])).astype(BF16)
    unshift = unshift.reshape(KF * rows, rows + 16)
    freq = jnp.arange(N2, dtype=jnp.int32)[:, None]
    angle = ((2 * (freq % LH) + 1) * tap_of[None, :]) % (2 * N2)
    angle = angle.astype(F32) * np.float32(np.pi / N2)
    fil_fwd = jnp.where(freq < LH, jnp.cos(angle), -jnp.sin(angle)).astype(BF16)

    feat, z = pl.pallas_call(
        feat_kernel,
        grid=grid,
        in_specs=[
            const_spec(shift.shape),
            stack_spec(3, rows, width),
            stack_spec(3, 16, width),
            stack_spec(3, KF, width),
        ],
        out_specs=[stack_spec(3, rows, width), rows_spec(rows, width)],
        out_shape=[
            jax.ShapeDtypeStruct((3, rows, chans), BF16),
            jax.ShapeDtypeStruct((rows, chans), BF16),
        ],
        scratch_shapes=[pltpu.VMEM((rows + 16, width), BF16)],
        name="feat",
    )(shift, streams, stream_rim, feat_taps)

    z_prev = passed_along(z, line, 1)
    q_next = passed_along(feat[0], line, -1)
    direction = score_dir[None, :]
    fwd = jnp.asarray(FWD)
    inv = jnp.asarray(INV)

    mixed, proj = pl.pallas_call(
        mix_kernel,
        grid_spec=pltpu.PrefetchScalarGridSpec(
            num_scalar_prefetch=1,
            grid=grid,
            in_specs=[
                const_spec((N2, N2)),
                const_spec((LH, N2)),
                const_spec((N2, LH)),
                const_spec((1, N2)),
                const_spec((rows, 1)),
                rows_spec(rows, width),
                rows_spec(rows, width),
                rows_spec(LH, width),
                stack_spec(1, rows, width),
                rows_spec(1, width),
            ],
            out_specs=[rows_spec(rows, width), const_spec((rows, 128))],
            scratch_shapes=[pltpu.VMEM((2 * rows, width), BF16)],
        ),
        out_shape=[
            jax.ShapeDtypeStruct((rows, chans), F32),
            jax.ShapeDtypeStruct((rows, 128), F32),
        ],
        name="mix",
    )(
        limits, fwd, inv[LH:], fil_fwd, seg_span[None, : 2 * rows], seg_now[:, None],
        z_prev, z, filt, feat, direction,
    )

    onehot = (seg_now[:, None] == jnp.arange(seg_count, dtype=jnp.int32)[None, :]).astype(F32)
    part = jnp.sum(onehot[:, :, None] * proj[:, None, :], axis=0)
    totals = jnp.sum(group_total(part, sizes), axis=1)
    coef = list_coef(totals, seg_lengths, list_ids)
    seg_on = seg_span[rows:]
    hot_on = seg_on[:, None] == jnp.arange(seg_count, dtype=jnp.int32)[None, :]
    tok_coef = jnp.sum(jnp.where(hot_on, coef[None, :], 0.0), axis=1)[:, None]

    grads, filter_part = pl.pallas_call(
        grad_kernel,
        grid_spec=pltpu.PrefetchScalarGridSpec(
            num_scalar_prefetch=1,
            grid=grid,
            in_specs=[
                const_spec((N2, N2)),
                const_spec((LH, N2)),
                const_spec((N2, LH)),
                const_spec((1, N2)),
                const_spec((rows, 1)),
                const_spec((2 * rows, 1)),
                rows_spec(rows, width),
                rows_spec(rows, width),
                rows_spec(rows, width),
                rows_spec(1, width),
                stack_spec(3, rows, width),
                rows_spec(rows, width),
                rows_spec(rows, width),
                rows_spec(LH, width),
            ],
            out_specs=[stack_spec(3, rows, width), rows_spec(LH, width)],
            scratch_shapes=[
                pltpu.VMEM((2 * rows, width), BF16),
                pltpu.VMEM((rows, width), F32),
                pltpu.VMEM((N2, width), F32),
            ],
        ),
        out_shape=[
            jax.ShapeDtypeStruct((3, rows, chans), BF16),
            jax.ShapeDtypeStruct((LH, chans), BF16),
        ],
        name="grad",
    )(
        limits, fwd, inv[:LH], fil_fwd, seg_on[None, :], seg_now[:, None], tok_coef, upstream,
        up_next, q_next, direction, feat, mixed, z, filt,
    )

    grad_rim = passed_along(grads[:, :16, :], line, -1)
    d_streams, taps_part = pl.pallas_call(
        back_kernel,
        grid=grid,
        in_specs=[
            const_spec(unshift.shape),
            stack_spec(3, rows, width),
            stack_spec(3, 16, width),
            stack_spec(3, rows, width),
            stack_spec(3, KF, width),
        ],
        out_specs=[stack_spec(3, rows, width), rows_spec(24, width)],
        out_shape=[
            jax.ShapeDtypeStruct((3, rows, chans), BF16),
            jax.ShapeDtypeStruct((24, chans), F32),
        ],
        scratch_shapes=[pltpu.VMEM((rows + 16, width), BF16)],
        name="back",
    )(unshift, grads, grad_rim, streams, feat_taps)

    shard_rows = long_filter.shape[0]
    sums = reduced(filter_part, taps_part, shard_rows)
    d_feat = sums[shard_rows:].reshape(3, 8, chans)[:, :KF, :]
    return (d_streams, d_feat, sums[:shard_rows])


def solution(mesh):
    placed = (
        P(None, ("groups", "ctx", "sub"), "fsdp"),
        P(None, None, "fsdp"),
        P("ctx", "fsdp"),
        P(("groups", "ctx", "sub"), "fsdp"),
        P("fsdp"),
        P("groups"),
        P("groups"),
    )
    sizes = (mesh.shape["ctx"], mesh.shape["fsdp"], mesh.shape["sub"])
    return jax.shard_map(
        functools.partial(local, sizes),
        mesh=mesh,
        in_specs=placed,
        out_specs=(
            P(None, ("groups", "ctx", "sub"), "fsdp"),
            P("groups", None, "fsdp"),
            P(("groups", "ctx"), "fsdp"),
        ),
        check_vma=False,
    )
```

```python
import functools

import jax
import jax.numpy as jnp
import numpy as np
from jax import lax
from jax.experimental import pallas as pl
from jax.experimental.pallas import tpu as pltpu
from jax.sharding import PartitionSpec as P

LH = 128
KF = 7
N2 = 2 * LH
F32 = jnp.float32
BF16 = jnp.bfloat16

_K, _N = np.meshgrid(np.arange(LH), np.arange(N2), indexing="ij")
_ANGLE = np.pi * (2 * _K + 1) * _N / N2
FWD = np.concatenate([np.cos(_ANGLE), -np.sin(_ANGLE)], axis=0).astype(np.float32)
INV = (FWD.T / LH).astype(np.float32)


def passed_along(value, axis, steps):
    count = lax.axis_size(axis)
    leading, last = (max(0, -steps), min(count, count - steps))
    return lax.ppermute(value, axis, [(source, source + steps) for source in range(leading, last)])


def segments_at(seg_lengths, positions):
    offsets = jnp.cumsum(seg_lengths, dtype=jnp.int32) - seg_lengths
    member = offsets[None, :] <= positions[:, None]
    seg_index = jnp.sum(member.astype(jnp.int32), axis=1, dtype=jnp.int32) - 1
    seg_start = jnp.max(jnp.where(member, offsets[None, :], 0), axis=1)
    return (seg_index, positions - seg_start)


def dot(a, b):
    return jnp.dot(a, b, preferred_element_type=F32)


MESH = pl.DeviceIdType.MESH


def place():
    group, ctx = lax.axis_index("groups"), lax.axis_index("ctx")
    fsdp, sub = lax.axis_index("fsdp"), lax.axis_index("sub")
    return group, ctx, fsdp, sub


def meet(n_ctx):
    group, ctx, fsdp, sub = place()
    line = ctx * 2 + sub
    barrier = pltpu.get_barrier_semaphore()
    left = (group, (line - 1) // 2, fsdp, 1 - sub)
    right = (group, (line + 1) // 2, fsdp, 1 - sub)

    @pl.when(line > 0)
    def _():
        pl.semaphore_signal(barrier, inc=1, device_id=left, device_id_type=MESH)

    @pl.when(line < 2 * n_ctx - 1)
    def _():
        pl.semaphore_signal(barrier, inc=1, device_id=right, device_id_type=MESH)

    pl.semaphore_signal(barrier, inc=1, device_id=(group, ctx, fsdp, 1 - sub), device_id_type=MESH)
    for r in range(1, n_ctx):
        pl.semaphore_signal(
            barrier, inc=1, device_id=(group, lax.rem(ctx + r, n_ctx), fsdp, sub),
            device_id_type=MESH,
        )
    ends = jnp.where(line > 0, 1, 0) + jnp.where(line < 2 * n_ctx - 1, 1, 0)
    pl.semaphore_wait(barrier, n_ctx + ends)
    return line > 0, line < 2 * n_ctx - 1, left, right


def send(src, dst, sems, device):
    return pltpu.make_async_remote_copy(
        src_ref=src, dst_ref=dst, send_sem=sems[0], recv_sem=sems[1], device_id=device,
        device_id_type=MESH,
    )


def feat_kernel(
    n_ctx, width, shift_ref, x_ref, taps_ref, fil_ref, feat_ref, z_ref, prev_ref, next_ref,
    all_ref, rim_ref, ext_ref, rim_sem, z_sem, q_sem, fil_sem, swap_sem,
):
    group, ctx, fsdp, sub = place()
    rows, chans = x_ref.shape[1:]
    blocks = chans // width
    has_left, has_right, left, right = meet(n_ctx)
    partner = (group, ctx, fsdp, 1 - sub)

    def rim_copy():
        return send(
            x_ref.at[:, pl.ds(rows - 16, 16), :], rim_ref, (rim_sem.at[0], rim_sem.at[1]), right
        )

    def columns(b):
        return pl.ds(pl.multiple_of(b * width, width), width)

    def z_copy(b):
        return send(
            z_ref.at[:, columns(b)], prev_ref.at[:, columns(b)], (z_sem.at[0, b], z_sem.at[1, b]),
            right,
        )

    def q_copy(b):
        return send(
            feat_ref.at[0, :, columns(b)], next_ref.at[:, columns(b)],
            (q_sem.at[0, b], q_sem.at[1, b]), left,
        )

    def fil_copy(r):
        return send(
            fil_ref.at[sub], all_ref.at[ctx, sub], (fil_sem.at[0, r], fil_sem.at[1, r]),
            (group, lax.rem(ctx + r, n_ctx), fsdp, sub),
        )

    def swap_copy(r):
        held = lax.rem(ctx - r + n_ctx, n_ctx)
        return send(
            all_ref.at[held, sub], all_ref.at[held, sub], (swap_sem.at[0, r], swap_sem.at[1, r]),
            partner,
        )

    @pl.when(has_right)
    def _():
        rim_copy().start()

    for r in range(1, n_ctx):
        fil_copy(r).start()
    all_ref[ctx] = fil_ref[...]

    @pl.when(jnp.logical_not(has_left))
    def _():
        rim_ref[...] = jnp.zeros(rim_ref.shape, BF16)
        prev_ref[...] = jnp.zeros(prev_ref.shape, BF16)

    @pl.when(jnp.logical_not(has_right))
    def _():
        next_ref[...] = jnp.zeros(next_ref.shape, BF16)

    @pl.when(has_left)
    def _():
        rim_copy().wait_recv()

    def block(b, carry):
        cols = columns(b)
        feats = [None] * 3
        for i in (1, 2, 0):
            ext_ref[i, 0:16, :] = rim_ref[i, :, cols]
            ext_ref[i, 16:, :] = x_ref[i, :, cols]
            ext = ext_ref[i]
            total = jnp.zeros((rows, width), F32)
            for j in range(KF):
                total = total + taps_ref[i, j : j + 1, cols] * dot(
                    shift_ref[j * rows : (j + 1) * rows, :], ext
                )
            feats[i] = total.astype(BF16)
            feat_ref[i, :, cols] = feats[i]
            if i == 2:
                z_ref[:, cols] = (feats[1].astype(F32) * feats[2].astype(F32)).astype(BF16)

        @pl.when(has_right)
        def _():
            z_copy(b).start()

        @pl.when(has_left)
        def _():
            q_copy(b).start()

        return carry

    lax.fori_loop(0, blocks, block, 0)

    for r in range(1, n_ctx):
        fil_copy(r).wait()
        swap_copy(r).start()

    @pl.when(has_right)
    def _():
        rim_copy().wait_send()
        for b in range(blocks):
            z_copy(b).wait_send()
            q_copy(b).wait_recv()

    @pl.when(has_left)
    def _():
        for b in range(blocks):
            z_copy(b).wait_recv()
            q_copy(b).wait_send()

    for r in range(1, n_ctx):
        swap_copy(r).wait()


def mix_kernel(
    span_ref, fwd_ref, inv_ref, fil_fwd_ref, colseg_ref, rowseg_ref, prev_ref, z_ref, fil_ref,
    q_ref, dir_ref, w_ref, proj_ref, ext_ref,
):
    rows = z_ref.shape[0]
    ext_ref[0:rows, :] = prev_ref[...]
    ext_ref[rows:, :] = z_ref[...]
    spec = dot(fil_fwd_ref[...], fil_ref[...])
    f_re, f_im = spec[:LH], spec[LH:]
    w_ref[...] = jnp.zeros(w_ref.shape, F32)

    def one(s, carry):
        fwd = jnp.where(colseg_ref[...] == s, fwd_ref[...], 0.0).astype(BF16)
        hat = dot(fwd, ext_ref[...])
        z_re, z_im = hat[:LH], hat[LH:]
        prod = jnp.concatenate(
            [(f_re * z_re - f_im * z_im).astype(BF16), (f_re * z_im + f_im * z_re).astype(BF16)],
            axis=0,
        )
        inv = jnp.where(rowseg_ref[...] == s, inv_ref[...], 0.0).astype(BF16)
        w_ref[...] += dot(inv, prod)
        return carry

    lax.fori_loop(span_ref[0], span_ref[1] + 1, one, 0)
    weighted = q_ref[0].astype(F32) * w_ref[...] * dir_ref[...]
    part = weighted[:, 0:128]
    for b in range(1, weighted.shape[1] // 128):
        part = part + weighted[:, b * 128 : (b + 1) * 128]

    @pl.when(pl.program_id(0) == 0)
    def _():
        proj_ref[...] = jnp.zeros(proj_ref.shape, F32)

    proj_ref[...] += part


def grad_kernel(
    span_ref, fwd_ref, inv_ref, fil_fwd_ref, colseg_ref, rowseg_ref, tokcoef_ref, up_ref,
    up_next_ref, q_next_ref, dir_ref, feat_ref, w_ref, z_ref, fil_ref,
    da_ref, dfil_ref, ext_ref, dz_ref, corr_ref,
):
    rows = z_ref.shape[0]
    d_out = up_ref[...].astype(F32) + tokcoef_ref[0:rows, :] * dir_ref[...]
    da_ref[0] = (d_out * w_ref[...]).astype(BF16)
    ext_ref[0:rows, :] = (d_out * feat_ref[0].astype(F32)).astype(BF16)
    d_next = up_next_ref[...].astype(F32) + tokcoef_ref[rows:, :] * dir_ref[...]
    ext_ref[rows:, :] = (d_next * q_next_ref[...].astype(F32)).astype(BF16)
    spec = dot(fil_fwd_ref[...], fil_ref[...])
    f_re, f_im = spec[:LH], spec[LH:]
    dz_ref[...] = jnp.zeros(dz_ref.shape, F32)
    corr_ref[...] = jnp.zeros(corr_ref.shape, F32)

    def one(s, carry):
        fwd = jnp.where(colseg_ref[...] == s, fwd_ref[...], 0.0).astype(BF16)
        hat = dot(fwd, ext_ref[...])
        d_re, d_im = hat[:LH], hat[LH:]
        prod = jnp.concatenate(
            [(f_re * d_re + f_im * d_im).astype(BF16), (f_re * d_im - f_im * d_re).astype(BF16)],
            axis=0,
        )
        inv = jnp.where(rowseg_ref[...] == s, inv_ref[...], 0.0).astype(BF16)
        dz_ref[...] += dot(inv, prod)
        zhat = dot(fwd[:, :rows], z_ref[...])
        z_re, z_im = zhat[:LH], zhat[LH:]
        corr_ref[:LH] += z_re * d_re + z_im * d_im
        corr_ref[LH:] += z_re * d_im - z_im * d_re
        return carry

    lax.fori_loop(span_ref[0], span_ref[1] + 1, one, 0)
    d_prod = dz_ref[...]
    da_ref[1] = (d_prod * feat_ref[2].astype(F32)).astype(BF16)
    da_ref[2] = (d_prod * feat_ref[1].astype(F32)).astype(BF16)
    dfil_ref[...] = dot(inv_ref[...].astype(BF16), corr_ref[...].astype(BF16)).astype(BF16)


def back_kernel(
    n_ctx, width, shift_ref, da_ref, x_ref, taps_ref, dfil_ref, dx_ref, dtaps_ref, out_ref,
    halo_ref, ext_ref, tap_ref, fil_a, fil_b, fil_c, fil_sum, tap_a, tap_b, tap_c, tap_sum,
    halo_sem, a_sem, b_sem, c_sem,
):
    group, ctx, fsdp, sub = place()
    rows, chans = x_ref.shape[1:]
    half = chans // 2
    has_left, has_right, left, right = meet(n_ctx)
    partner = (group, ctx, fsdp, 1 - sub)
    kept = pl.ds(pl.multiple_of(sub * half, half), half)
    given = pl.ds(pl.multiple_of((1 - sub) * half, half), half)

    def halo_copy():
        return send(
            da_ref.at[:, pl.ds(0, 16), :], halo_ref, (halo_sem.at[0], halo_sem.at[1]), left
        )

    first = [send(dfil_ref.at[:, :, given], fil_a, (a_sem.at[0, 0], a_sem.at[1, 0]), partner)]
    for i in range(3):
        first.append(
            send(
                tap_ref.at[i, :, given], tap_a.at[i], (a_sem.at[0, 1 + i], a_sem.at[1, 1 + i]),
                partner,
            )
        )

    def second(c, r):
        sems = (b_sem.at[0, c, r], b_sem.at[1, c, r])
        owner = lax.rem(ctx + r, n_ctx)
        target = (group, owner, fsdp, sub)
        if c == 0:
            return send(fil_c.at[owner], fil_b.at[r], sems, target)
        return send(tap_c.at[c - 1], tap_b.at[r, c - 1], sems, target)

    last = [
        send(fil_sum, out_ref.at[:, kept], (c_sem.at[0, 0], c_sem.at[1, 0]), partner),
        send(tap_sum, dtaps_ref.at[:, :, kept], (c_sem.at[0, 1], c_sem.at[1, 1]), partner),
    ]

    @pl.when(has_left)
    def _():
        halo_copy().start()

    first[0].start()

    @pl.when(jnp.logical_not(has_right))
    def _():
        halo_ref[...] = jnp.zeros(halo_ref.shape, BF16)

    @pl.when(has_right)
    def _():
        halo_copy().wait_recv()

    def stream(i):
        def block(b, carry):
            cols = pl.ds(pl.multiple_of(b * width, width), width)
            ext_ref[0:rows, :] = da_ref[i, :, cols]
            ext_ref[rows:, :] = halo_ref[i, :, cols]
            ext = ext_ref[...]
            own = x_ref[i, :, cols].astype(F32)
            total = jnp.zeros((rows, width), F32)
            sums = []
            for j in range(KF):
                moved = dot(shift_ref[j * rows : (j + 1) * rows, :], ext)
                total = total + taps_ref[i, j : j + 1, cols] * moved
                sums.append(jnp.sum(own * moved, axis=0, keepdims=True))
            sums.append(jnp.zeros((1, width), F32))
            tap_ref[i, :, cols] = jnp.concatenate(sums, axis=0).astype(BF16)
            dx_ref[i, :, cols] = total.astype(BF16)
            return carry

        lax.fori_loop(0, chans // width, block, 0)

    def relay(c):
        first[c].wait()
        if c == 0:
            fil_c[...] = (dfil_ref[:, :, kept].astype(F32) + fil_a[...].astype(F32)).astype(BF16)
        else:
            i = c - 1
            tap_c[i] = (tap_ref[i, :, kept].astype(F32) + tap_a[i].astype(F32)).astype(BF16)
        for r in range(1, n_ctx):
            second(c, r).start()

    stream(0)
    first[1].start()
    relay(0)
    stream(1)
    first[2].start()
    relay(1)
    stream(2)
    first[3].start()
    relay(2)
    for r in range(1, n_ctx):
        second(0, r).wait()
    total = fil_c[ctx].astype(F32)
    for r in range(1, n_ctx):
        total = total + fil_b[r].astype(F32)
    fil_sum[...] = total
    out_ref[:, kept] = total
    relay(3)
    last[0].start()
    for c in range(1, 4):
        for r in range(1, n_ctx):
            second(c, r).wait()
    tap_b[0] = tap_c[...]

    def add(d, running):
        return running + tap_b[lax.rem(ctx - d + n_ctx, n_ctx)].astype(F32)

    taps_total = lax.fori_loop(0, n_ctx, add, jnp.zeros(tap_sum.shape, F32))
    tap_sum[...] = taps_total
    dtaps_ref[:, :, kept] = taps_total
    last[1].start()
    last[0].wait()
    last[1].wait()

    @pl.when(has_left)
    def _():
        halo_copy().wait_send()


def const_spec(shape):
    return pl.BlockSpec(shape, lambda b, *_: (0,) * len(shape))


def rows_spec(rows, width):
    return pl.BlockSpec((rows, width), lambda b, *_: (0, b))


def stack_spec(count, rows, width):
    return pl.BlockSpec((count, rows, width), lambda b, *_: (0, 0, b))


def total_kernel(
    sizes, proj_ref, seg_ref, on_ref, lens_ref, ids_ref, ids_row_ref, out_ref, part_ref, slots,
    send_sem, recv_sem,
):
    n_ctx, n_fsdp, n_sub = sizes
    count = n_ctx * n_fsdp * n_sub
    me = (lax.axis_index("ctx") * n_fsdp + lax.axis_index("fsdp")) * n_sub + lax.axis_index("sub")
    group = lax.axis_index("groups")

    def where(r):
        peer = lax.rem(me + r, count)
        return (
            group,
            peer // (n_fsdp * n_sub),
            lax.rem(peer // n_sub, n_fsdp),
            lax.rem(peer, n_sub),
        )

    barrier = pltpu.get_barrier_semaphore()

    def greet(r, carry):
        pl.semaphore_signal(
            barrier, inc=1, device_id=where(r), device_id_type=pl.DeviceIdType.MESH
        )
        return carry

    lax.fori_loop(1, count, greet, 0)
    segs = part_ref.shape[0]
    for s in range(segs):
        part_ref[s : s + 1, :] = jnp.sum(
            jnp.where(seg_ref[...] == s, proj_ref[...], 0.0), axis=0, keepdims=True
        )
    pl.semaphore_wait(barrier, count - 1)

    def copy(r):
        return pltpu.make_async_remote_copy(
            src_ref=part_ref,
            dst_ref=slots.at[r],
            send_sem=send_sem.at[r],
            recv_sem=recv_sem.at[r],
            device_id=where(r),
            device_id_type=pl.DeviceIdType.MESH,
        )

    def begin(r, carry):
        copy(r).start()
        return carry

    def end(r, carry):
        copy(r).wait()
        return carry

    lax.fori_loop(1, count, begin, 0)
    lax.fori_loop(1, count, end, 0)
    slots[0] = part_ref[...]

    def add(i, total):
        return total + slots[lax.rem(me - i + count, count)]

    summed = lax.fori_loop(0, count, add, jnp.zeros(part_ref.shape, F32))
    lengths = lens_ref[...].astype(F32)
    scores = jnp.sum(summed, axis=1, keepdims=True) / lengths
    down = lax.broadcasted_iota(jnp.int32, (segs, segs), 0)
    across = lax.broadcasted_iota(jnp.int32, (segs, segs), 1)
    same = down == across
    score_row = jnp.sum(jnp.where(same, scores, 0.0), axis=0, keepdims=True)
    mates = jnp.where(ids_ref[...] == ids_row_ref[...], 1.0, 0.0)
    means = jnp.sum(mates * score_row, axis=1, keepdims=True) / jnp.sum(
        mates, axis=1, keepdims=True
    )
    coef = (scores - means) / lengths
    coef_row = jnp.sum(jnp.where(same, coef, 0.0), axis=0, keepdims=True)
    wide = (on_ref.shape[0], segs)
    hot = on_ref[...] == lax.broadcasted_iota(jnp.int32, wide, 1)
    out_ref[...] = jnp.sum(jnp.where(hot, coef_row, 0.0), axis=1, keepdims=True)


def token_coef(sizes, proj, seg_now, seg_on, seg_lengths, list_ids):
    count = sizes[0] * sizes[1] * sizes[2]
    segs = seg_lengths.shape[0]
    return pl.pallas_call(
        functools.partial(total_kernel, sizes),
        out_shape=jax.ShapeDtypeStruct((seg_on.shape[0], 1), F32),
        in_specs=[pl.BlockSpec(memory_space=pltpu.VMEM)] * 6,
        out_specs=pl.BlockSpec(memory_space=pltpu.VMEM),
        scratch_shapes=[
            pltpu.VMEM((segs, 128), F32),
            pltpu.VMEM((count, segs, 128), F32),
            pltpu.SemaphoreType.DMA((count,)),
            pltpu.SemaphoreType.DMA((count,)),
        ],
        compiler_params=pltpu.CompilerParams(collective_id=0, has_side_effects=True),
        name="token_coef",
    )(proj, seg_now[:, None], seg_on[:, None], seg_lengths[:, None], list_ids[:, None],
      list_ids[None, :])


def local(sizes, streams, feat_taps, long_filter, upstream, score_dir, seg_lengths, list_ids):
    rows, chans = streams.shape[1:]
    seg_count = seg_lengths.shape[0]
    width = min(512, chans)
    grid = (chans // width,)
    line = ("ctx", "sub")

    n_ctx = sizes[0]
    shard_rows = long_filter.shape[0]
    vmem = pl.BlockSpec(memory_space=pltpu.VMEM)
    dma = pltpu.SemaphoreType.DMA

    first_row = lax.axis_index(line) * rows
    positions = first_row - rows + jnp.arange(3 * rows, dtype=jnp.int32)
    seg_span, age_span = segments_at(seg_lengths, positions)
    age_now = age_span[rows : 2 * rows]
    age_on = age_span[rows:]
    seg_now = seg_span[rows : 2 * rows]
    limits = jnp.stack([seg_now[0], seg_now[rows - 1]])
    taps = jnp.arange(KF, dtype=jnp.int32)[:, None, None]
    at = jnp.arange(rows, dtype=jnp.int32)[None, :, None]
    spot = jnp.arange(rows + 16, dtype=jnp.int32)[None, None, :]
    shift = ((spot == 16 + at - taps) & (taps <= age_now[None, :, None])).astype(BF16)
    shift = shift.reshape(KF * rows, rows + 16)
    unshift = ((spot == at + taps) & (taps <= age_on[None, None, : rows + 16])).astype(BF16)
    unshift = unshift.reshape(KF * rows, rows + 16)
    fwd = jnp.asarray(FWD)
    inv = jnp.asarray(INV)
    fil_fwd = jnp.asarray(FWD[:, :LH], BF16)

    blocks = chans // width
    feat, z, z_prev, q_next, filt = pl.pallas_call(
        functools.partial(feat_kernel, n_ctx, width),
        in_specs=[vmem] * 4,
        out_specs=[vmem] * 5,
        out_shape=[
            jax.ShapeDtypeStruct((3, rows, chans), BF16),
            jax.ShapeDtypeStruct((rows, chans), BF16),
            jax.ShapeDtypeStruct((rows, chans), BF16),
            jax.ShapeDtypeStruct((rows, chans), BF16),
            jax.ShapeDtypeStruct((n_ctx, 2, shard_rows // 2, chans), BF16),
        ],
        scratch_shapes=[
            pltpu.VMEM((3, 16, chans), BF16),
            pltpu.VMEM((3, rows + 16, width), BF16),
            dma((2,)),
            dma((2, blocks)),
            dma((2, blocks)),
            dma((2, n_ctx)),
            dma((2, n_ctx)),
        ],
        compiler_params=pltpu.CompilerParams(collective_id=1, has_side_effects=True),
        name="feat",
    )(shift, streams, feat_taps, long_filter.reshape(2, shard_rows // 2, chans))
    filt = filt.reshape(LH, chans)
    up_next = passed_along(upstream, line, -1)
    direction = score_dir[None, :]

    mixed, proj = pl.pallas_call(
        mix_kernel,
        grid_spec=pltpu.PrefetchScalarGridSpec(
            num_scalar_prefetch=1,
            grid=grid,
            in_specs=[
                const_spec((N2, N2)),
                const_spec((LH, N2)),
                const_spec((N2, LH)),
                const_spec((1, N2)),
                const_spec((rows, 1)),
                rows_spec(rows, width),
                rows_spec(rows, width),
                rows_spec(LH, width),
                stack_spec(1, rows, width),
                rows_spec(1, width),
            ],
            out_specs=[rows_spec(rows, width), const_spec((rows, 128))],
            scratch_shapes=[pltpu.VMEM((2 * rows, width), BF16)],
        ),
        out_shape=[
            jax.ShapeDtypeStruct((rows, chans), F32),
            jax.ShapeDtypeStruct((rows, 128), F32),
        ],
        name="mix",
    )(
        limits, fwd, inv[LH:], fil_fwd, seg_span[None, : 2 * rows], seg_now[:, None],
        z_prev, z, filt, feat, direction,
    )

    seg_on = seg_span[rows:]
    tok_coef = token_coef(sizes, proj, seg_now, seg_on, seg_lengths, list_ids)

    grads, filter_part = pl.pallas_call(
        grad_kernel,
        grid_spec=pltpu.PrefetchScalarGridSpec(
            num_scalar_prefetch=1,
            grid=grid,
            in_specs=[
                const_spec((N2, N2)),
                const_spec((LH, N2)),
                const_spec((N2, LH)),
                const_spec((1, N2)),
                const_spec((rows, 1)),
                const_spec((2 * rows, 1)),
                rows_spec(rows, width),
                rows_spec(rows, width),
                rows_spec(rows, width),
                rows_spec(1, width),
                stack_spec(3, rows, width),
                rows_spec(rows, width),
                rows_spec(rows, width),
                rows_spec(LH, width),
            ],
            out_specs=[stack_spec(3, rows, width), rows_spec(LH, width)],
            scratch_shapes=[
                pltpu.VMEM((2 * rows, width), BF16),
                pltpu.VMEM((rows, width), F32),
                pltpu.VMEM((N2, width), F32),
            ],
        ),
        out_shape=[
            jax.ShapeDtypeStruct((3, rows, chans), BF16),
            jax.ShapeDtypeStruct((LH, chans), BF16),
        ],
        name="grad",
    )(
        limits, fwd, inv[:LH], fil_fwd, seg_on[None, :], seg_now[:, None], tok_coef, upstream,
        up_next, q_next, direction, feat, mixed, z, filt,
    )

    half = chans // 2
    d_streams, d_taps, d_filter = pl.pallas_call(
        functools.partial(back_kernel, n_ctx, width),
        in_specs=[vmem] * 5,
        out_specs=[vmem] * 3,
        out_shape=[
            jax.ShapeDtypeStruct((3, rows, chans), BF16),
            jax.ShapeDtypeStruct((3, 8, chans), F32),
            jax.ShapeDtypeStruct((shard_rows, chans), F32),
        ],
        scratch_shapes=[
            pltpu.VMEM((3, 16, chans), BF16),
            pltpu.VMEM((rows + 16, width), BF16),
            pltpu.VMEM((3, 8, chans), BF16),
            pltpu.VMEM((n_ctx, shard_rows, half), BF16),
            pltpu.VMEM((n_ctx, shard_rows, half), BF16),
            pltpu.VMEM((n_ctx, shard_rows, half), BF16),
            pltpu.VMEM((shard_rows, half), F32),
            pltpu.VMEM((3, 8, half), BF16),
            pltpu.VMEM((n_ctx, 3, 8, half), BF16),
            pltpu.VMEM((3, 8, half), BF16),
            pltpu.VMEM((3, 8, half), F32),
            dma((2,)),
            dma((2, 4)),
            dma((2, 4, n_ctx)),
            dma((2, 2)),
        ],
        compiler_params=pltpu.CompilerParams(collective_id=2, has_side_effects=True),
        name="back",
    )(unshift, grads, streams, feat_taps, filter_part.reshape(n_ctx, shard_rows, chans))
    return (d_streams, d_taps[:, :KF, :], d_filter)


def solution(mesh):
    placed = (
        P(None, ("groups", "ctx", "sub"), "fsdp"),
        P(None, None, "fsdp"),
        P("ctx", "fsdp"),
        P(("groups", "ctx", "sub"), "fsdp"),
        P("fsdp"),
        P("groups"),
        P("groups"),
    )
    sizes = (mesh.shape["ctx"], mesh.shape["fsdp"], mesh.shape["sub"])
    return jax.shard_map(
        functools.partial(local, sizes),
        mesh=mesh,
        in_specs=placed,
        out_specs=(
            P(None, ("groups", "ctx", "sub"), "fsdp"),
            P("groups", None, "fsdp"),
            P(("groups", "ctx"), "fsdp"),
        ),
        check_vma=False,
    )
```

```python
import functools

import jax
import jax.numpy as jnp
import numpy as np
from jax import lax
from jax.experimental import pallas as pl
from jax.experimental.pallas import tpu as pltpu
from jax.sharding import PartitionSpec as P

LH = 128
KF = 7
N2 = 2 * LH
F32 = jnp.float32
BF16 = jnp.bfloat16

_K, _N = np.meshgrid(np.arange(LH), np.arange(N2), indexing="ij")
_ANGLE = np.pi * (2 * _K + 1) * _N / N2
FWD = np.concatenate([np.cos(_ANGLE), -np.sin(_ANGLE)], axis=0).astype(np.float32)
INV = (FWD.T / LH).astype(np.float32)


def starts(lens_ref):
    offsets, off = [], jnp.int32(0)
    for s in range(lens_ref.shape[0]):
        offsets.append(off)
        off = off + lens_ref[s]
    return offsets


def segment_of(offsets, position):
    seg = jnp.where(offsets[0] <= position, 0, -1)
    for off in offsets[1:]:
        seg = seg + jnp.where(off <= position, 1, 0)
    return seg


def age_of(offsets, position):
    start = jnp.zeros(position.shape, jnp.int32)
    for off in offsets:
        start = jnp.where(off <= position, off, start)
    return position - start


def first_token(rows):
    return (lax.axis_index("ctx") * 2 + lax.axis_index("sub")) * rows


def down(rows):
    return lax.broadcasted_iota(jnp.int32, (rows, 1), 0)


def across(columns):
    return lax.broadcasted_iota(jnp.int32, (1, columns), 1)


def dot(a, b):
    return jnp.dot(a, b, preferred_element_type=F32)


MESH = pl.DeviceIdType.MESH


def place():
    group, ctx = lax.axis_index("groups"), lax.axis_index("ctx")
    fsdp, sub = lax.axis_index("fsdp"), lax.axis_index("sub")
    return group, ctx, fsdp, sub


def meet(n_ctx):
    group, ctx, fsdp, sub = place()
    line = ctx * 2 + sub
    barrier = pltpu.get_barrier_semaphore()
    left = (group, (line - 1) // 2, fsdp, 1 - sub)
    right = (group, (line + 1) // 2, fsdp, 1 - sub)

    @pl.when(line > 0)
    def _():
        pl.semaphore_signal(barrier, inc=1, device_id=left, device_id_type=MESH)

    @pl.when(line < 2 * n_ctx - 1)
    def _():
        pl.semaphore_signal(barrier, inc=1, device_id=right, device_id_type=MESH)

    pl.semaphore_signal(barrier, inc=1, device_id=(group, ctx, fsdp, 1 - sub), device_id_type=MESH)
    for r in range(1, n_ctx):
        pl.semaphore_signal(
            barrier, inc=1, device_id=(group, lax.rem(ctx + r, n_ctx), fsdp, sub),
            device_id_type=MESH,
        )
    ends = jnp.where(line > 0, 1, 0) + jnp.where(line < 2 * n_ctx - 1, 1, 0)
    pl.semaphore_wait(barrier, n_ctx + ends)
    return line > 0, line < 2 * n_ctx - 1, left, right


def send(src, dst, sems, device):
    return pltpu.make_async_remote_copy(
        src_ref=src, dst_ref=dst, send_sem=sems[0], recv_sem=sems[1], device_id=device,
        device_id_type=MESH,
    )


def feat_kernel(
    n_ctx, width, lens_ref, x_ref, taps_ref, fil_ref, up_ref, feat_ref, z_ref, prev_ref, next_ref,
    all_ref, shift_ref, rim_ref, ext_ref, rim_sem, z_sem, up_sem, fil_sem, swap_sem,
):
    group, ctx, fsdp, sub = place()
    rows, chans = x_ref.shape[1:]
    blocks = chans // width
    has_left, has_right, left, right = meet(n_ctx)
    partner = (group, ctx, fsdp, 1 - sub)

    def rim_copy():
        return send(
            x_ref.at[:, pl.ds(rows - 16, 16), :], rim_ref, (rim_sem.at[0], rim_sem.at[1]), right
        )

    def columns(b):
        return pl.ds(pl.multiple_of(b * width, width), width)

    def z_copy(b):
        return send(
            z_ref.at[:, columns(b)], prev_ref.at[:, columns(b)], (z_sem.at[0, b], z_sem.at[1, b]),
            right,
        )

    def up_copy():
        return send(up_ref, next_ref, (up_sem.at[0], up_sem.at[1]), left)

    def fil_copy(r):
        return send(
            fil_ref.at[sub], all_ref.at[ctx, sub], (fil_sem.at[0, r], fil_sem.at[1, r]),
            (group, lax.rem(ctx + r, n_ctx), fsdp, sub),
        )

    def swap_copy(r):
        held = lax.rem(ctx - r + n_ctx, n_ctx)
        return send(
            all_ref.at[held, sub], all_ref.at[held, sub], (swap_sem.at[0, r], swap_sem.at[1, r]),
            partner,
        )

    @pl.when(has_right)
    def _():
        rim_copy().start()

    for r in range(1, n_ctx):
        fil_copy(r).start()

    @pl.when(has_left)
    def _():
        up_copy().start()

    all_ref[ctx] = fil_ref[...]
    age = age_of(starts(lens_ref), first_token(rows) + down(rows))
    gap = across(rows + 16) - down(rows) - 16
    for j in range(KF):
        shift_ref[j * rows : (j + 1) * rows, :] = jnp.where(
            (gap == -j) & (age >= j), 1.0, 0.0
        ).astype(BF16)

    @pl.when(jnp.logical_not(has_left))
    def _():
        rim_ref[...] = jnp.zeros(rim_ref.shape, BF16)
        prev_ref[...] = jnp.zeros(prev_ref.shape, BF16)

    @pl.when(jnp.logical_not(has_right))
    def _():
        next_ref[...] = jnp.zeros(next_ref.shape, BF16)

    @pl.when(has_left)
    def _():
        rim_copy().wait_recv()

    def block(b, carry):
        cols = columns(b)
        feats = [None] * 3
        for i in (1, 2, 0):
            ext_ref[i, 0:16, :] = rim_ref[i, :, cols]
            ext_ref[i, 16:, :] = x_ref[i, :, cols]
            ext = ext_ref[i]
            total = jnp.zeros((rows, width), F32)
            for j in range(KF):
                total = total + taps_ref[i, j : j + 1, cols] * dot(
                    shift_ref[j * rows : (j + 1) * rows, :], ext
                )
            feats[i] = total.astype(BF16)
            feat_ref[i, :, cols] = feats[i]
            if i == 2:
                z_ref[:, cols] = (feats[1].astype(F32) * feats[2].astype(F32)).astype(BF16)

        @pl.when(has_right)
        def _():
            z_copy(b).start()

        return carry

    lax.fori_loop(0, blocks, block, 0)

    for r in range(1, n_ctx):
        fil_copy(r).wait()
        swap_copy(r).start()

    @pl.when(has_right)
    def _():
        rim_copy().wait_send()
        for b in range(blocks):
            z_copy(b).wait_send()
        up_copy().wait_recv()

    @pl.when(has_left)
    def _():
        for b in range(blocks):
            z_copy(b).wait_recv()
        up_copy().wait_send()

    for r in range(1, n_ctx):
        swap_copy(r).wait()


def mix_kernel(
    lens_ref, fwd_ref, inv_ref, fil_fwd_ref, prev_ref, z_ref, fil_ref, q_ref, dir_ref, w_ref, proj_ref, ext_ref,
):
    rows = z_ref.shape[0]
    offsets, base = starts(lens_ref), first_token(rows)
    colseg = segment_of(offsets, base - rows + across(2 * rows))
    rowseg = segment_of(offsets, base + down(rows))
    ext_ref[0:rows, :] = prev_ref[...]
    ext_ref[rows:, :] = z_ref[...]
    spec = dot(fil_fwd_ref[...], fil_ref[...])
    f_re, f_im = spec[:LH], spec[LH:]
    w_ref[...] = jnp.zeros(w_ref.shape, F32)

    def one(s, carry):
        fwd = jnp.where(colseg == s, fwd_ref[...], 0.0).astype(BF16)
        hat = dot(fwd, ext_ref[...])
        z_re, z_im = hat[:LH], hat[LH:]
        prod = jnp.concatenate(
            [(f_re * z_re - f_im * z_im).astype(BF16), (f_re * z_im + f_im * z_re).astype(BF16)],
            axis=0,
        )
        inv = jnp.where(rowseg == s, inv_ref[...], 0.0).astype(BF16)
        w_ref[...] += dot(inv, prod)
        return carry

    lowest, highest = segment_of(offsets, base), segment_of(offsets, base + rows - 1)
    lax.fori_loop(lowest, highest + 1, one, 0)
    weighted = q_ref[0].astype(F32) * w_ref[...] * dir_ref[...]
    part = weighted[:, 0:128]
    for b in range(1, weighted.shape[1] // 128):
        part = part + weighted[:, b * 128 : (b + 1) * 128]

    @pl.when(pl.program_id(0) == 0)
    def _():
        proj_ref[...] = jnp.zeros(proj_ref.shape, F32)

    proj_ref[...] += part


def grad_kernel(
    lens_ref, fwd_ref, inv_ref, fil_fwd_ref, tokcoef_ref, up_ref,
    up_next_ref, q_next_ref, dir_ref, feat_ref, w_ref, z_ref, fil_ref,
    da_ref, dfil_ref, ext_ref, dz_ref, corr_ref,
):
    rows = z_ref.shape[0]
    offsets, base = starts(lens_ref), first_token(rows)
    colseg = segment_of(offsets, base + across(2 * rows))
    rowseg = segment_of(offsets, base + down(rows))
    d_out = up_ref[...].astype(F32) + tokcoef_ref[0:rows, :] * dir_ref[...]
    da_ref[0] = (d_out * w_ref[...]).astype(BF16)
    ext_ref[0:rows, :] = (d_out * feat_ref[0].astype(F32)).astype(BF16)
    d_next = up_next_ref[...].astype(F32) + tokcoef_ref[rows:, :] * dir_ref[...]
    ext_ref[rows:, :] = (d_next * q_next_ref[...].astype(F32)).astype(BF16)
    spec = dot(fil_fwd_ref[...], fil_ref[...])
    f_re, f_im = spec[:LH], spec[LH:]
    dz_ref[...] = jnp.zeros(dz_ref.shape, F32)
    corr_ref[...] = jnp.zeros(corr_ref.shape, F32)

    def one(s, carry):
        fwd = jnp.where(colseg == s, fwd_ref[...], 0.0).astype(BF16)
        hat = dot(fwd, ext_ref[...])
        d_re, d_im = hat[:LH], hat[LH:]
        prod = jnp.concatenate(
            [(f_re * d_re + f_im * d_im).astype(BF16), (f_re * d_im - f_im * d_re).astype(BF16)],
            axis=0,
        )
        inv = jnp.where(rowseg == s, inv_ref[...], 0.0).astype(BF16)
        dz_ref[...] += dot(inv, prod)
        zhat = dot(fwd[:, :rows], z_ref[...])
        z_re, z_im = zhat[:LH], zhat[LH:]
        corr_ref[:LH] += z_re * d_re + z_im * d_im
        corr_ref[LH:] += z_re * d_im - z_im * d_re
        return carry

    lowest, highest = segment_of(offsets, base), segment_of(offsets, base + rows - 1)
    lax.fori_loop(lowest, highest + 1, one, 0)
    d_prod = dz_ref[...]
    da_ref[1] = (d_prod * feat_ref[2].astype(F32)).astype(BF16)
    da_ref[2] = (d_prod * feat_ref[1].astype(F32)).astype(BF16)
    dfil_ref[...] = dot(inv_ref[...].astype(BF16), corr_ref[...].astype(BF16)).astype(BF16)


def back_kernel(
    n_ctx, width, lens_ref, da_ref, x_ref, taps_ref, dfil_ref, dx_ref, dtaps_ref, out_ref,
    shift_ref, halo_ref, ext_ref, tap_ref, fil_a, fil_b, fil_c, fil_sum, tap_a, tap_b, tap_c, tap_sum,
    halo_sem, a_sem, b_sem, c_sem,
):
    group, ctx, fsdp, sub = place()
    rows, chans = x_ref.shape[1:]
    half = chans // 2
    has_left, has_right, left, right = meet(n_ctx)
    partner = (group, ctx, fsdp, 1 - sub)
    kept = pl.ds(pl.multiple_of(sub * half, half), half)
    given = pl.ds(pl.multiple_of((1 - sub) * half, half), half)

    def halo_copy():
        return send(
            da_ref.at[:, pl.ds(0, 16), :], halo_ref, (halo_sem.at[0], halo_sem.at[1]), left
        )

    first = [send(dfil_ref.at[:, :, given], fil_a, (a_sem.at[0, 0], a_sem.at[1, 0]), partner)]
    for i in range(3):
        first.append(
            send(
                tap_ref.at[i, :, given], tap_a.at[i], (a_sem.at[0, 1 + i], a_sem.at[1, 1 + i]),
                partner,
            )
        )

    def second(c, r):
        sems = (b_sem.at[0, c, r], b_sem.at[1, c, r])
        owner = lax.rem(ctx + r, n_ctx)
        target = (group, owner, fsdp, sub)
        if c == 0:
            return send(fil_c.at[owner], fil_b.at[r], sems, target)
        return send(tap_c.at[c - 1], tap_b.at[r, c - 1], sems, target)

    last = [
        send(fil_sum, out_ref.at[:, kept], (c_sem.at[0, 0], c_sem.at[1, 0]), partner),
        send(tap_sum, dtaps_ref.at[:, :, kept], (c_sem.at[0, 1], c_sem.at[1, 1]), partner),
    ]

    @pl.when(has_left)
    def _():
        halo_copy().start()

    first[0].start()

    @pl.when(jnp.logical_not(has_right))
    def _():
        halo_ref[...] = jnp.zeros(halo_ref.shape, BF16)

    age = age_of(starts(lens_ref), first_token(rows) + across(rows + 16))
    gap = across(rows + 16) - down(rows)
    for j in range(KF):
        shift_ref[j * rows : (j + 1) * rows, :] = jnp.where(
            (gap == j) & (age >= j), 1.0, 0.0
        ).astype(BF16)

    @pl.when(has_right)
    def _():
        halo_copy().wait_recv()

    def stream(i):
        def block(b, carry):
            cols = pl.ds(pl.multiple_of(b * width, width), width)
            ext_ref[0:rows, :] = da_ref[i, :, cols]
            ext_ref[rows:, :] = halo_ref[i, :, cols]
            ext = ext_ref[...]
            own = x_ref[i, :, cols].astype(F32)
            total = jnp.zeros((rows, width), F32)
            sums = []
            for j in range(KF):
                moved = dot(shift_ref[j * rows : (j + 1) * rows, :], ext)
                total = total + taps_ref[i, j : j + 1, cols] * moved
                sums.append(jnp.sum(own * moved, axis=0, keepdims=True))
            sums.append(jnp.zeros((1, width), F32))
            tap_ref[i, :, cols] = jnp.concatenate(sums, axis=0).astype(BF16)
            dx_ref[i, :, cols] = total.astype(BF16)
            return carry

        lax.fori_loop(0, chans // width, block, 0)

    def relay(c):
        first[c].wait()
        if c == 0:
            fil_c[...] = (dfil_ref[:, :, kept].astype(F32) + fil_a[...].astype(F32)).astype(BF16)
        else:
            i = c - 1
            tap_c[i] = (tap_ref[i, :, kept].astype(F32) + tap_a[i].astype(F32)).astype(BF16)
        for r in range(1, n_ctx):
            second(c, r).start()

    stream(0)
    first[1].start()
    relay(0)
    stream(1)
    first[2].start()
    relay(1)
    stream(2)
    first[3].start()
    relay(2)
    for r in range(1, n_ctx):
        second(0, r).wait()
    total = fil_c[ctx].astype(F32)
    for r in range(1, n_ctx):
        total = total + fil_b[r].astype(F32)
    fil_sum[...] = total
    out_ref[:, kept] = total
    relay(3)
    last[0].start()
    for c in range(1, 4):
        for r in range(1, n_ctx):
            second(c, r).wait()
    tap_b[0] = tap_c[...]

    def add(d, running):
        return running + tap_b[lax.rem(ctx - d + n_ctx, n_ctx)].astype(F32)

    taps_total = lax.fori_loop(0, n_ctx, add, jnp.zeros(tap_sum.shape, F32))
    tap_sum[...] = taps_total
    dtaps_ref[:, :, kept] = taps_total
    last[1].start()
    last[0].wait()
    last[1].wait()

    @pl.when(has_left)
    def _():
        halo_copy().wait_send()


def const_spec(shape):
    return pl.BlockSpec(shape, lambda b, *_: (0,) * len(shape))


def rows_spec(rows, width):
    return pl.BlockSpec((rows, width), lambda b, *_: (0, b))


def stack_spec(count, rows, width):
    return pl.BlockSpec((count, rows, width), lambda b, *_: (0, 0, b))


def total_kernel(
    sizes, lens_ref, ids_ref, proj_ref, feat_ref, out_ref, next_ref, part_ref, slots, send_sem,
    recv_sem, q_sem,
):
    n_ctx, n_fsdp, n_sub = sizes
    count = n_ctx * n_fsdp * n_sub
    me = (lax.axis_index("ctx") * n_fsdp + lax.axis_index("fsdp")) * n_sub + lax.axis_index("sub")
    group = lax.axis_index("groups")

    def where(r):
        peer = lax.rem(me + r, count)
        return (
            group,
            peer // (n_fsdp * n_sub),
            lax.rem(peer // n_sub, n_fsdp),
            lax.rem(peer, n_sub),
        )

    barrier = pltpu.get_barrier_semaphore()

    def greet(r, carry):
        pl.semaphore_signal(
            barrier, inc=1, device_id=where(r), device_id_type=pl.DeviceIdType.MESH
        )
        return carry

    lax.fori_loop(1, count, greet, 0)
    segs, rows = part_ref.shape[0], proj_ref.shape[0]
    offsets, base = starts(lens_ref), first_token(rows)
    rowseg = segment_of(offsets, base + down(rows))
    for s in range(segs):
        part_ref[s : s + 1, :] = jnp.sum(
            jnp.where(rowseg == s, proj_ref[...], 0.0), axis=0, keepdims=True
        )
    pl.semaphore_wait(barrier, count - 1)

    def copy(r):
        return pltpu.make_async_remote_copy(
            src_ref=part_ref,
            dst_ref=slots.at[r],
            send_sem=send_sem.at[r],
            recv_sem=recv_sem.at[r],
            device_id=where(r),
            device_id_type=pl.DeviceIdType.MESH,
        )

    def begin(r, carry):
        copy(r).start()
        return carry

    def end(r, carry):
        copy(r).wait()
        return carry

    _, ctx, fsdp, sub = place()
    line = ctx * 2 + sub
    q_copy = send(
        feat_ref.at[0], next_ref, (q_sem.at[0], q_sem.at[1]), (group, (line - 1) // 2, fsdp, 1 - sub)
    )
    lax.fori_loop(1, count, begin, 0)

    @pl.when(line > 0)
    def _():
        q_copy.start()

    @pl.when(line == 2 * n_ctx - 1)
    def _():
        next_ref[...] = jnp.zeros(next_ref.shape, BF16)

    lax.fori_loop(1, count, end, 0)
    slots[0] = part_ref[...]

    def add(i, total):
        return total + slots[lax.rem(me - i + count, count)]

    summed = lax.fori_loop(0, count, add, jnp.zeros(part_ref.shape, F32))
    ids, id_row = jnp.zeros((segs, 1), jnp.int32), jnp.zeros((1, segs), jnp.int32)
    lengths = jnp.zeros((segs, 1), jnp.int32)
    for s in range(segs):
        ids = jnp.where(down(segs) == s, ids_ref[s], ids)
        id_row = jnp.where(across(segs) == s, ids_ref[s], id_row)
        lengths = jnp.where(down(segs) == s, lens_ref[s], lengths)
    lengths = lengths.astype(F32)
    scores = jnp.sum(summed, axis=1, keepdims=True) / lengths
    same = down(segs) == across(segs)
    score_row = jnp.sum(jnp.where(same, scores, 0.0), axis=0, keepdims=True)
    mates = jnp.where(ids == id_row, 1.0, 0.0)
    means = jnp.sum(mates * score_row, axis=1, keepdims=True) / jnp.sum(
        mates, axis=1, keepdims=True
    )
    coef = (scores - means) / lengths
    coef_row = jnp.sum(jnp.where(same, coef, 0.0), axis=0, keepdims=True)
    hot = segment_of(offsets, base + down(2 * rows)) == across(segs)
    out_ref[...] = jnp.sum(jnp.where(hot, coef_row, 0.0), axis=1, keepdims=True)

    @pl.when(line > 0)
    def _():
        q_copy.wait_send()

    @pl.when(line < 2 * n_ctx - 1)
    def _():
        q_copy.wait_recv()


def token_coef(sizes, seg_lengths, list_ids, proj, feat):
    count = sizes[0] * sizes[1] * sizes[2]
    segs = seg_lengths.shape[0]
    rows, chans = feat.shape[1:]
    smem = pl.BlockSpec(memory_space=pltpu.SMEM)
    vmem = pl.BlockSpec(memory_space=pltpu.VMEM)
    return pl.pallas_call(
        functools.partial(total_kernel, sizes),
        out_shape=[
            jax.ShapeDtypeStruct((2 * rows, 1), F32), jax.ShapeDtypeStruct((rows, chans), BF16)
        ],
        in_specs=[smem, smem, vmem, pl.BlockSpec(memory_space=pl.ANY)],
        out_specs=[vmem, vmem],
        scratch_shapes=[
            pltpu.VMEM((segs, 128), F32),
            pltpu.VMEM((count, segs, 128), F32),
            pltpu.SemaphoreType.DMA((count,)),
            pltpu.SemaphoreType.DMA((count,)),
            pltpu.SemaphoreType.DMA((2,)),
        ],
        compiler_params=pltpu.CompilerParams(collective_id=0, has_side_effects=True),
        name="token_coef",
    )(seg_lengths, list_ids, proj, feat)


def local(sizes, streams, feat_taps, long_filter, upstream, score_dir, seg_lengths, list_ids):
    rows, chans = streams.shape[1:]
    width = min(512, chans)
    grid = (chans // width,)

    n_ctx = sizes[0]
    shard_rows = long_filter.shape[0]
    vmem = pl.BlockSpec(memory_space=pltpu.VMEM)
    smem = pl.BlockSpec(memory_space=pltpu.SMEM)
    dma = pltpu.SemaphoreType.DMA

    fwd = jnp.asarray(FWD)
    inv = jnp.asarray(INV)
    fil_fwd = jnp.asarray(FWD[:, :LH], BF16)

    blocks = chans // width
    feat, z, z_prev, up_next, filt = pl.pallas_call(
        functools.partial(feat_kernel, n_ctx, width),
        in_specs=[smem, vmem, vmem, vmem, pl.BlockSpec(memory_space=pl.ANY)],
        out_specs=[vmem] * 5,
        out_shape=[
            jax.ShapeDtypeStruct((3, rows, chans), BF16),
            jax.ShapeDtypeStruct((rows, chans), BF16),
            jax.ShapeDtypeStruct((rows, chans), BF16),
            jax.ShapeDtypeStruct((rows, chans), BF16),
            jax.ShapeDtypeStruct((n_ctx, 2, shard_rows // 2, chans), BF16),
        ],
        scratch_shapes=[
            pltpu.VMEM((KF * rows, rows + 16), BF16),
            pltpu.VMEM((3, 16, chans), BF16),
            pltpu.VMEM((3, rows + 16, width), BF16),
            dma((2,)),
            dma((2, blocks)),
            dma((2,)),
            dma((2, n_ctx)),
            dma((2, n_ctx)),
        ],
        compiler_params=pltpu.CompilerParams(collective_id=1, has_side_effects=True),
        name="feat",
    )(seg_lengths, streams, feat_taps, long_filter.reshape(2, shard_rows // 2, chans), upstream)
    filt = filt.reshape(LH, chans)
    direction = score_dir[None, :]

    mixed, proj = pl.pallas_call(
        mix_kernel,
        grid_spec=pltpu.PrefetchScalarGridSpec(
            num_scalar_prefetch=1,
            grid=grid,
            in_specs=[
                const_spec((N2, N2)),
                const_spec((LH, N2)),
                const_spec((N2, LH)),
                rows_spec(rows, width),
                rows_spec(rows, width),
                rows_spec(LH, width),
                stack_spec(1, rows, width),
                rows_spec(1, width),
            ],
            out_specs=[rows_spec(rows, width), const_spec((rows, 128))],
            scratch_shapes=[pltpu.VMEM((2 * rows, width), BF16)],
        ),
        out_shape=[
            jax.ShapeDtypeStruct((rows, chans), F32),
            jax.ShapeDtypeStruct((rows, 128), F32),
        ],
        name="mix",
    )(
        seg_lengths, fwd, inv[LH:], fil_fwd, z_prev, z, filt, feat, direction,
    )

    tok_coef, q_next = token_coef(sizes, seg_lengths, list_ids, proj, feat)

    grads, filter_part = pl.pallas_call(
        grad_kernel,
        grid_spec=pltpu.PrefetchScalarGridSpec(
            num_scalar_prefetch=1,
            grid=grid,
            in_specs=[
                const_spec((N2, N2)),
                const_spec((LH, N2)),
                const_spec((N2, LH)),
                const_spec((2 * rows, 1)),
                rows_spec(rows, width),
                rows_spec(rows, width),
                rows_spec(rows, width),
                rows_spec(1, width),
                stack_spec(3, rows, width),
                rows_spec(rows, width),
                rows_spec(rows, width),
                rows_spec(LH, width),
            ],
            out_specs=[stack_spec(3, rows, width), rows_spec(LH, width)],
            scratch_shapes=[
                pltpu.VMEM((2 * rows, width), BF16),
                pltpu.VMEM((rows, width), F32),
                pltpu.VMEM((N2, width), F32),
            ],
        ),
        out_shape=[
            jax.ShapeDtypeStruct((3, rows, chans), BF16),
            jax.ShapeDtypeStruct((LH, chans), BF16),
        ],
        name="grad",
    )(
        seg_lengths, fwd, inv[:LH], fil_fwd, tok_coef, upstream,
        up_next, q_next, direction, feat, mixed, z, filt,
    )

    half = chans // 2
    d_streams, d_taps, d_filter = pl.pallas_call(
        functools.partial(back_kernel, n_ctx, width),
        in_specs=[smem] + [vmem] * 4,
        out_specs=[vmem] * 3,
        out_shape=[
            jax.ShapeDtypeStruct((3, rows, chans), BF16),
            jax.ShapeDtypeStruct((3, 8, chans), F32),
            jax.ShapeDtypeStruct((shard_rows, chans), F32),
        ],
        scratch_shapes=[
            pltpu.VMEM((KF * rows, rows + 16), BF16),
            pltpu.VMEM((3, 16, chans), BF16),
            pltpu.VMEM((rows + 16, width), BF16),
            pltpu.VMEM((3, 8, chans), BF16),
            pltpu.VMEM((n_ctx, shard_rows, half), BF16),
            pltpu.VMEM((n_ctx, shard_rows, half), BF16),
            pltpu.VMEM((n_ctx, shard_rows, half), BF16),
            pltpu.VMEM((shard_rows, half), F32),
            pltpu.VMEM((3, 8, half), BF16),
            pltpu.VMEM((n_ctx, 3, 8, half), BF16),
            pltpu.VMEM((3, 8, half), BF16),
            pltpu.VMEM((3, 8, half), F32),
            dma((2,)),
            dma((2, 4)),
            dma((2, 4, n_ctx)),
            dma((2, 2)),
        ],
        compiler_params=pltpu.CompilerParams(collective_id=2, has_side_effects=True),
        name="back",
    )(seg_lengths, grads, streams, feat_taps, filter_part.reshape(n_ctx, shard_rows, chans))
    return (d_streams, d_taps[:, :KF, :], d_filter)


def solution(mesh):
    placed = (
        P(None, ("groups", "ctx", "sub"), "fsdp"),
        P(None, None, "fsdp"),
        P("ctx", "fsdp"),
        P(("groups", "ctx", "sub"), "fsdp"),
        P("fsdp"),
        P("groups"),
        P("groups"),
    )
    sizes = (mesh.shape["ctx"], mesh.shape["fsdp"], mesh.shape["sub"])
    return jax.shard_map(
        functools.partial(local, sizes),
        mesh=mesh,
        in_specs=placed,
        out_specs=(
            P(None, ("groups", "ctx", "sub"), "fsdp"),
            P("groups", None, "fsdp"),
            P(("groups", "ctx"), "fsdp"),
        ),
        check_vma=False,
    )
```

```python
import functools

import jax
import jax.numpy as jnp
import numpy as np
from jax import lax
from jax.experimental import pallas as pl
from jax.experimental.pallas import tpu as pltpu
from jax.sharding import PartitionSpec as P

LH = 128
KF = 7
N2 = 2 * LH
F32 = jnp.float32
BF16 = jnp.bfloat16

_K, _N = np.meshgrid(np.arange(LH), np.arange(N2), indexing="ij")
_ANGLE = np.pi * (2 * _K + 1) * _N / N2
FWD = np.concatenate([np.cos(_ANGLE), -np.sin(_ANGLE)], axis=0).astype(np.float32)
INV = (FWD.T / LH).astype(np.float32)


def starts(lens_ref):
    offsets, off = [], jnp.int32(0)
    for s in range(lens_ref.shape[0]):
        offsets.append(off)
        off = off + lens_ref[s]
    return offsets


def segment_of(offsets, position):
    seg = jnp.where(offsets[0] <= position, 0, -1)
    for off in offsets[1:]:
        seg = seg + jnp.where(off <= position, 1, 0)
    return seg


def age_of(offsets, position):
    start = jnp.zeros(position.shape, jnp.int32)
    for off in offsets:
        start = jnp.where(off <= position, off, start)
    return position - start


def first_token(rows):
    return (lax.axis_index("ctx") * 2 + lax.axis_index("sub")) * rows


def down(rows):
    return lax.broadcasted_iota(jnp.int32, (rows, 1), 0)


def across(columns):
    return lax.broadcasted_iota(jnp.int32, (1, columns), 1)


def dot(a, b):
    return jnp.dot(a, b, preferred_element_type=F32)


MESH = pl.DeviceIdType.MESH


def place():
    group, ctx = lax.axis_index("groups"), lax.axis_index("ctx")
    fsdp, sub = lax.axis_index("fsdp"), lax.axis_index("sub")
    return group, ctx, fsdp, sub


def meet(n_ctx):
    group, ctx, fsdp, sub = place()
    line = ctx * 2 + sub
    barrier = pltpu.get_barrier_semaphore()
    left = (group, (line - 1) // 2, fsdp, 1 - sub)
    right = (group, (line + 1) // 2, fsdp, 1 - sub)

    @pl.when(line > 0)
    def _():
        pl.semaphore_signal(barrier, inc=1, device_id=left, device_id_type=MESH)

    @pl.when(line < 2 * n_ctx - 1)
    def _():
        pl.semaphore_signal(barrier, inc=1, device_id=right, device_id_type=MESH)

    pl.semaphore_signal(barrier, inc=1, device_id=(group, ctx, fsdp, 1 - sub), device_id_type=MESH)
    for r in range(1, n_ctx):
        pl.semaphore_signal(
            barrier, inc=1, device_id=(group, lax.rem(ctx + r, n_ctx), fsdp, sub),
            device_id_type=MESH,
        )
    ends = jnp.where(line > 0, 1, 0) + jnp.where(line < 2 * n_ctx - 1, 1, 0)
    pl.semaphore_wait(barrier, n_ctx + ends)
    return line > 0, line < 2 * n_ctx - 1, left, right


def send(src, dst, sems, device):
    return pltpu.make_async_remote_copy(
        src_ref=src, dst_ref=dst, send_sem=sems[0], recv_sem=sems[1], device_id=device,
        device_id_type=MESH,
    )


def feat_kernel(
    n_ctx, width, lens_ref, x_ref, taps_ref, fil_ref, up_ref, feat_ref, z_ref, prev_ref, next_ref,
    all_ref, rim_ref, shift_ref, ext_ref, rim_sem, z_sem, up_sem, fil_sem, swap_sem,
):
    group, ctx, fsdp, sub = place()
    rows, chans = x_ref.shape[1:]
    blocks = chans // width
    has_left, has_right, left, right = meet(n_ctx)
    partner = (group, ctx, fsdp, 1 - sub)

    def rim_copy():
        return send(
            x_ref.at[:, pl.ds(rows - 16, 16), :], rim_ref, (rim_sem.at[0], rim_sem.at[1]), right
        )

    def columns(b):
        return pl.ds(pl.multiple_of(b * width, width), width)

    def z_copy(b):
        return send(
            z_ref.at[:, columns(b)], prev_ref.at[:, columns(b)], (z_sem.at[0, b], z_sem.at[1, b]),
            right,
        )

    def up_copy():
        return send(up_ref, next_ref, (up_sem.at[0], up_sem.at[1]), left)

    def fil_copy(r):
        return send(
            fil_ref.at[sub], all_ref.at[ctx, sub], (fil_sem.at[0, r], fil_sem.at[1, r]),
            (group, lax.rem(ctx + r, n_ctx), fsdp, sub),
        )

    def swap_copy(r):
        held = lax.rem(ctx - r + n_ctx, n_ctx)
        return send(
            all_ref.at[held, sub], all_ref.at[held, sub], (swap_sem.at[0, r], swap_sem.at[1, r]),
            partner,
        )

    @pl.when(has_right)
    def _():
        rim_copy().start()

    for r in range(1, n_ctx):
        fil_copy(r).start()

    @pl.when(has_left)
    def _():
        up_copy().start()

    all_ref[ctx] = fil_ref[...]
    age = age_of(starts(lens_ref), first_token(rows) + down(rows))
    gap = across(rows + 16) - down(rows) - 16
    for j in range(KF):
        shift_ref[j * rows : (j + 1) * rows, :] = jnp.where(
            (gap == -j) & (age >= j), 1.0, 0.0
        ).astype(BF16)

    @pl.when(jnp.logical_not(has_left))
    def _():
        rim_ref[...] = jnp.zeros(rim_ref.shape, BF16)
        prev_ref[...] = jnp.zeros(prev_ref.shape, BF16)

    @pl.when(jnp.logical_not(has_right))
    def _():
        next_ref[...] = jnp.zeros(next_ref.shape, BF16)

    @pl.when(has_left)
    def _():
        rim_copy().wait_recv()

    def block(b, carry):
        cols = columns(b)
        feats = [None] * 3
        for i in (1, 2, 0):
            ext_ref[i, 0:16, :] = rim_ref[i, :, cols]
            ext_ref[i, 16:, :] = x_ref[i, :, cols]
            ext = ext_ref[i]
            total = jnp.zeros((rows, width), F32)
            for j in range(KF):
                total = total + taps_ref[i, j : j + 1, cols] * dot(
                    shift_ref[j * rows : (j + 1) * rows, :], ext
                )
            feats[i] = total.astype(BF16)
            feat_ref[i, :, cols] = feats[i]
            if i == 2:
                z_ref[:, cols] = (feats[1].astype(F32) * feats[2].astype(F32)).astype(BF16)

        @pl.when(has_right)
        def _():
            z_copy(b).start()

        return carry

    lax.fori_loop(0, blocks, block, 0)

    for r in range(1, n_ctx):
        fil_copy(r).wait()
        swap_copy(r).start()

    @pl.when(has_right)
    def _():
        rim_copy().wait_send()
        for b in range(blocks):
            z_copy(b).wait_send()
        up_copy().wait_recv()

    @pl.when(has_left)
    def _():
        for b in range(blocks):
            z_copy(b).wait_recv()
        up_copy().wait_send()

    for r in range(1, n_ctx):
        swap_copy(r).wait()


def mix_kernel(
    lens_ref, fwd_ref, inv_ref, fil_fwd_ref, prev_ref, z_ref, fil_ref, q_ref, dir_ref, w_ref, proj_ref, ext_ref,
):
    rows = z_ref.shape[0]
    offsets, base = starts(lens_ref), first_token(rows)
    colseg = segment_of(offsets, base - rows + across(2 * rows))
    rowseg = segment_of(offsets, base + down(rows))
    ext_ref[0:rows, :] = prev_ref[...]
    ext_ref[rows:, :] = z_ref[...]
    spec = dot(fil_fwd_ref[...], fil_ref[...])
    f_re, f_im = spec[:LH], spec[LH:]
    w_ref[...] = jnp.zeros(w_ref.shape, F32)

    def one(s, carry):
        fwd = jnp.where(colseg == s, fwd_ref[...], 0.0).astype(BF16)
        hat = dot(fwd, ext_ref[...])
        z_re, z_im = hat[:LH], hat[LH:]
        prod = jnp.concatenate(
            [(f_re * z_re - f_im * z_im).astype(BF16), (f_re * z_im + f_im * z_re).astype(BF16)],
            axis=0,
        )
        inv = jnp.where(rowseg == s, inv_ref[...], 0.0).astype(BF16)
        w_ref[...] += dot(inv, prod)
        return carry

    lowest, highest = segment_of(offsets, base), segment_of(offsets, base + rows - 1)
    lax.fori_loop(lowest, highest + 1, one, 0)
    weighted = q_ref[0].astype(F32) * w_ref[...] * dir_ref[...]
    part = weighted[:, 0:128]
    for b in range(1, weighted.shape[1] // 128):
        part = part + weighted[:, b * 128 : (b + 1) * 128]

    @pl.when(pl.program_id(0) == 0)
    def _():
        proj_ref[...] = jnp.zeros(proj_ref.shape, F32)

    proj_ref[...] += part


def grad_kernel(
    lens_ref, fwd_ref, inv_ref, fil_fwd_ref, tokcoef_ref, up_ref,
    up_next_ref, q_next_ref, dir_ref, feat_ref, w_ref, z_ref, fil_ref,
    da_ref, dfil_ref, ext_ref, dz_ref, corr_ref,
):
    rows = z_ref.shape[0]
    offsets, base = starts(lens_ref), first_token(rows)
    colseg = segment_of(offsets, base + across(2 * rows))
    rowseg = segment_of(offsets, base + down(rows))
    d_out = up_ref[...].astype(F32) + tokcoef_ref[0:rows, :] * dir_ref[...]
    da_ref[0] = (d_out * w_ref[...]).astype(BF16)
    ext_ref[0:rows, :] = (d_out * feat_ref[0].astype(F32)).astype(BF16)
    d_next = up_next_ref[...].astype(F32) + tokcoef_ref[rows:, :] * dir_ref[...]
    ext_ref[rows:, :] = (d_next * q_next_ref[...].astype(F32)).astype(BF16)
    spec = dot(fil_fwd_ref[...], fil_ref[...])
    f_re, f_im = spec[:LH], spec[LH:]
    dz_ref[...] = jnp.zeros(dz_ref.shape, F32)
    corr_ref[...] = jnp.zeros(corr_ref.shape, F32)

    def one(s, carry):
        fwd = jnp.where(colseg == s, fwd_ref[...], 0.0).astype(BF16)
        hat = dot(fwd, ext_ref[...])
        d_re, d_im = hat[:LH], hat[LH:]
        prod = jnp.concatenate(
            [(f_re * d_re + f_im * d_im).astype(BF16), (f_re * d_im - f_im * d_re).astype(BF16)],
            axis=0,
        )
        inv = jnp.where(rowseg == s, inv_ref[...], 0.0).astype(BF16)
        dz_ref[...] += dot(inv, prod)
        zhat = dot(fwd[:, :rows], z_ref[...])
        z_re, z_im = zhat[:LH], zhat[LH:]
        corr_ref[:LH] += z_re * d_re + z_im * d_im
        corr_ref[LH:] += z_re * d_im - z_im * d_re
        return carry

    lowest, highest = segment_of(offsets, base), segment_of(offsets, base + rows - 1)
    lax.fori_loop(lowest, highest + 1, one, 0)
    d_prod = dz_ref[...]
    da_ref[1] = (d_prod * feat_ref[2].astype(F32)).astype(BF16)
    da_ref[2] = (d_prod * feat_ref[1].astype(F32)).astype(BF16)
    dfil_ref[...] = dot(inv_ref[...].astype(BF16), corr_ref[...].astype(BF16)).astype(BF16)


def back_kernel(
    n_ctx, width, lens_ref, da_ref, x_ref, rim_ref, taps_ref, dfil_ref, dx_ref, dtaps_ref, out_ref,
    shift_ref, halo_ref, ext_ref, tap_ref, fil_a, fil_b, fil_c, fil_sum, tap_a, tap_b, tap_c, tap_sum,
    halo_sem, a_sem, b_sem, c_sem,
):
    group, ctx, fsdp, sub = place()
    rows, chans = x_ref.shape[1:]
    half = chans // 2
    has_left, has_right, left, right = meet(n_ctx)
    partner = (group, ctx, fsdp, 1 - sub)
    kept = pl.ds(pl.multiple_of(sub * half, half), half)
    given = pl.ds(pl.multiple_of((1 - sub) * half, half), half)

    def halo_copy():
        return send(
            da_ref.at[:, pl.ds(0, 16), :], halo_ref, (halo_sem.at[0], halo_sem.at[1]), left
        )

    first = [send(dfil_ref.at[:, :, given], fil_a, (a_sem.at[0, 0], a_sem.at[1, 0]), partner)]
    for i in range(3):
        first.append(
            send(
                tap_ref.at[i, :, given], tap_a.at[i], (a_sem.at[0, 1 + i], a_sem.at[1, 1 + i]),
                partner,
            )
        )

    def second(c, r):
        sems = (b_sem.at[0, c, r], b_sem.at[1, c, r])
        owner = lax.rem(ctx + r, n_ctx)
        target = (group, owner, fsdp, sub)
        if c == 0:
            return send(fil_c.at[owner], fil_b.at[r], sems, target)
        return send(tap_c.at[c - 1], tap_b.at[r, c - 1], sems, target)

    last = [
        send(fil_sum, out_ref.at[:, kept], (c_sem.at[0, 0], c_sem.at[1, 0]), partner),
        send(tap_sum, dtaps_ref.at[:, :, kept], (c_sem.at[0, 1], c_sem.at[1, 1]), partner),
    ]

    @pl.when(has_left)
    def _():
        halo_copy().start()

    first[0].start()

    @pl.when(jnp.logical_not(has_right))
    def _():
        halo_ref[...] = jnp.zeros(halo_ref.shape, BF16)

    offsets, base = starts(lens_ref), first_token(rows)
    age = age_of(offsets, base + down(rows))
    gap = across(rows + 16) - down(rows)
    for j in range(KF):
        shift_ref[j * rows : (j + 1) * rows, :] = jnp.where(
            (gap == 16 - j) & (age >= j), 1.0, 0.0
        ).astype(BF16)

    def columns(b):
        return pl.ds(pl.multiple_of(b * width, width), width)

    def tap_sums(i):
        def block(b, carry):
            cols = columns(b)
            ext_ref[0:16, :] = rim_ref[i, :, cols]
            ext_ref[16:, :] = x_ref[i, :, cols]
            ext = ext_ref[...]
            own = da_ref[i, :, cols].astype(F32)
            sums = []
            for j in range(KF):
                moved = dot(shift_ref[j * rows : (j + 1) * rows, :], ext)
                sums.append(jnp.sum(own * moved, axis=0, keepdims=True))
            sums.append(jnp.zeros((1, width), F32))
            tap_ref[i, :, cols] = jnp.concatenate(sums, axis=0).astype(BF16)
            return carry

        lax.fori_loop(0, chans // width, block, 0)

    def stream(i):
        def block(b, carry):
            cols = columns(b)
            ext_ref[0:rows, :] = da_ref[i, :, cols]
            ext_ref[rows:, :] = halo_ref[i, :, cols]
            ext = ext_ref[...]
            total = jnp.zeros((rows, width), F32)
            for j in range(KF):
                total = total + taps_ref[i, j : j + 1, cols] * dot(
                    shift_ref[j * rows : (j + 1) * rows, :], ext
                )
            dx_ref[i, :, cols] = total.astype(BF16)
            return carry

        lax.fori_loop(0, chans // width, block, 0)

    def relay(c):
        first[c].wait()
        if c == 0:
            fil_c[...] = (dfil_ref[:, :, kept].astype(F32) + fil_a[...].astype(F32)).astype(BF16)
        else:
            i = c - 1
            tap_c[i] = (tap_ref[i, :, kept].astype(F32) + tap_a[i].astype(F32)).astype(BF16)
        for r in range(1, n_ctx):
            second(c, r).start()

    tap_sums(0)
    first[1].start()
    relay(0)
    tap_sums(1)
    first[2].start()
    relay(1)
    tap_sums(2)
    first[3].start()
    relay(2)
    age = age_of(offsets, base + across(rows + 16))
    for j in range(KF):
        shift_ref[j * rows : (j + 1) * rows, :] = jnp.where(
            (gap == j) & (age >= j), 1.0, 0.0
        ).astype(BF16)

    @pl.when(has_right)
    def _():
        halo_copy().wait_recv()

    stream(0)
    relay(3)
    stream(1)
    for r in range(1, n_ctx):
        second(0, r).wait()
    total = fil_c[ctx].astype(F32)
    for r in range(1, n_ctx):
        total = total + fil_b[r].astype(F32)
    fil_sum[...] = total
    out_ref[:, kept] = total
    last[0].start()
    stream(2)
    for c in range(1, 4):
        for r in range(1, n_ctx):
            second(c, r).wait()
    tap_b[0] = tap_c[...]

    def add(d, running):
        return running + tap_b[lax.rem(ctx - d + n_ctx, n_ctx)].astype(F32)

    taps_total = lax.fori_loop(0, n_ctx, add, jnp.zeros(tap_sum.shape, F32))
    tap_sum[...] = taps_total
    dtaps_ref[:, :, kept] = taps_total
    last[1].start()
    last[0].wait()
    last[1].wait()

    @pl.when(has_left)
    def _():
        halo_copy().wait_send()


def const_spec(shape):
    return pl.BlockSpec(shape, lambda b, *_: (0,) * len(shape))


def rows_spec(rows, width):
    return pl.BlockSpec((rows, width), lambda b, *_: (0, b))


def stack_spec(count, rows, width):
    return pl.BlockSpec((count, rows, width), lambda b, *_: (0, 0, b))


def total_kernel(
    sizes, lens_ref, ids_ref, proj_ref, feat_ref, out_ref, next_ref, part_ref, slots, send_sem,
    recv_sem, q_sem,
):
    n_ctx, n_fsdp, n_sub = sizes
    count = n_ctx * n_fsdp * n_sub
    me = (lax.axis_index("ctx") * n_fsdp + lax.axis_index("fsdp")) * n_sub + lax.axis_index("sub")
    group = lax.axis_index("groups")

    def where(r):
        peer = lax.rem(me + r, count)
        return (
            group,
            peer // (n_fsdp * n_sub),
            lax.rem(peer // n_sub, n_fsdp),
            lax.rem(peer, n_sub),
        )

    barrier = pltpu.get_barrier_semaphore()

    def greet(r, carry):
        pl.semaphore_signal(
            barrier, inc=1, device_id=where(r), device_id_type=pl.DeviceIdType.MESH
        )
        return carry

    lax.fori_loop(1, count, greet, 0)
    segs, rows = part_ref.shape[0], proj_ref.shape[0]
    offsets, base = starts(lens_ref), first_token(rows)
    rowseg = segment_of(offsets, base + down(rows))
    for s in range(segs):
        part_ref[s : s + 1, :] = jnp.sum(
            jnp.where(rowseg == s, proj_ref[...], 0.0), axis=0, keepdims=True
        )
    pl.semaphore_wait(barrier, count - 1)

    def copy(r):
        return pltpu.make_async_remote_copy(
            src_ref=part_ref,
            dst_ref=slots.at[r],
            send_sem=send_sem.at[r],
            recv_sem=recv_sem.at[r],
            device_id=where(r),
            device_id_type=pl.DeviceIdType.MESH,
        )

    def begin(r, carry):
        copy(r).start()
        return carry

    def end(r, carry):
        copy(r).wait()
        return carry

    _, ctx, fsdp, sub = place()
    line = ctx * 2 + sub
    q_copy = send(
        feat_ref.at[0], next_ref, (q_sem.at[0], q_sem.at[1]), (group, (line - 1) // 2, fsdp, 1 - sub)
    )
    lax.fori_loop(1, count, begin, 0)

    @pl.when(line > 0)
    def _():
        q_copy.start()

    @pl.when(line == 2 * n_ctx - 1)
    def _():
        next_ref[...] = jnp.zeros(next_ref.shape, BF16)

    lax.fori_loop(1, count, end, 0)
    slots[0] = part_ref[...]

    def add(i, total):
        return total + slots[lax.rem(me - i + count, count)]

    summed = lax.fori_loop(0, count, add, jnp.zeros(part_ref.shape, F32))
    ids, id_row = jnp.zeros((segs, 1), jnp.int32), jnp.zeros((1, segs), jnp.int32)
    lengths = jnp.zeros((segs, 1), jnp.int32)
    for s in range(segs):
        ids = jnp.where(down(segs) == s, ids_ref[s], ids)
        id_row = jnp.where(across(segs) == s, ids_ref[s], id_row)
        lengths = jnp.where(down(segs) == s, lens_ref[s], lengths)
    lengths = lengths.astype(F32)
    scores = jnp.sum(summed, axis=1, keepdims=True) / lengths
    same = down(segs) == across(segs)
    score_row = jnp.sum(jnp.where(same, scores, 0.0), axis=0, keepdims=True)
    mates = jnp.where(ids == id_row, 1.0, 0.0)
    means = jnp.sum(mates * score_row, axis=1, keepdims=True) / jnp.sum(
        mates, axis=1, keepdims=True
    )
    coef = (scores - means) / lengths
    coef_row = jnp.sum(jnp.where(same, coef, 0.0), axis=0, keepdims=True)
    hot = segment_of(offsets, base + down(2 * rows)) == across(segs)
    out_ref[...] = jnp.sum(jnp.where(hot, coef_row, 0.0), axis=1, keepdims=True)

    @pl.when(line > 0)
    def _():
        q_copy.wait_send()

    @pl.when(line < 2 * n_ctx - 1)
    def _():
        q_copy.wait_recv()


def token_coef(sizes, seg_lengths, list_ids, proj, feat):
    count = sizes[0] * sizes[1] * sizes[2]
    segs = seg_lengths.shape[0]
    rows, chans = feat.shape[1:]
    smem = pl.BlockSpec(memory_space=pltpu.SMEM)
    vmem = pl.BlockSpec(memory_space=pltpu.VMEM)
    return pl.pallas_call(
        functools.partial(total_kernel, sizes),
        out_shape=[
            jax.ShapeDtypeStruct((2 * rows, 1), F32), jax.ShapeDtypeStruct((rows, chans), BF16)
        ],
        in_specs=[smem, smem, vmem, pl.BlockSpec(memory_space=pl.ANY)],
        out_specs=[vmem, vmem],
        scratch_shapes=[
            pltpu.VMEM((segs, 128), F32),
            pltpu.VMEM((count, segs, 128), F32),
            pltpu.SemaphoreType.DMA((count,)),
            pltpu.SemaphoreType.DMA((count,)),
            pltpu.SemaphoreType.DMA((2,)),
        ],
        compiler_params=pltpu.CompilerParams(collective_id=0, has_side_effects=True),
        name="token_coef",
    )(seg_lengths, list_ids, proj, feat)


def local(sizes, streams, feat_taps, long_filter, upstream, score_dir, seg_lengths, list_ids):
    rows, chans = streams.shape[1:]
    width = min(512, chans)
    grid = (chans // width,)

    n_ctx = sizes[0]
    shard_rows = long_filter.shape[0]
    vmem = pl.BlockSpec(memory_space=pltpu.VMEM)
    smem = pl.BlockSpec(memory_space=pltpu.SMEM)
    dma = pltpu.SemaphoreType.DMA

    fwd = jnp.asarray(FWD)
    inv = jnp.asarray(INV)
    fil_fwd = jnp.asarray(FWD[:, :LH], BF16)

    blocks = chans // width
    feat, z, z_prev, up_next, filt, rim = pl.pallas_call(
        functools.partial(feat_kernel, n_ctx, width),
        in_specs=[smem, vmem, vmem, vmem, pl.BlockSpec(memory_space=pl.ANY)],
        out_specs=[vmem] * 6,
        out_shape=[
            jax.ShapeDtypeStruct((3, rows, chans), BF16),
            jax.ShapeDtypeStruct((rows, chans), BF16),
            jax.ShapeDtypeStruct((rows, chans), BF16),
            jax.ShapeDtypeStruct((rows, chans), BF16),
            jax.ShapeDtypeStruct((n_ctx, 2, shard_rows // 2, chans), BF16),
            jax.ShapeDtypeStruct((3, 16, chans), BF16),
        ],
        scratch_shapes=[
            pltpu.VMEM((KF * rows, rows + 16), BF16),
            pltpu.VMEM((3, rows + 16, width), BF16),
            dma((2,)),
            dma((2, blocks)),
            dma((2,)),
            dma((2, n_ctx)),
            dma((2, n_ctx)),
        ],
        compiler_params=pltpu.CompilerParams(collective_id=1, has_side_effects=True),
        name="feat",
    )(seg_lengths, streams, feat_taps, long_filter.reshape(2, shard_rows // 2, chans), upstream)
    filt = filt.reshape(LH, chans)
    direction = score_dir[None, :]

    mixed, proj = pl.pallas_call(
        mix_kernel,
        grid_spec=pltpu.PrefetchScalarGridSpec(
            num_scalar_prefetch=1,
            grid=grid,
            in_specs=[
                const_spec((N2, N2)),
                const_spec((LH, N2)),
                const_spec((N2, LH)),
                rows_spec(rows, width),
                rows_spec(rows, width),
                rows_spec(LH, width),
                stack_spec(1, rows, width),
                rows_spec(1, width),
            ],
            out_specs=[rows_spec(rows, width), const_spec((rows, 128))],
            scratch_shapes=[pltpu.VMEM((2 * rows, width), BF16)],
        ),
        out_shape=[
            jax.ShapeDtypeStruct((rows, chans), F32),
            jax.ShapeDtypeStruct((rows, 128), F32),
        ],
        name="mix",
    )(
        seg_lengths, fwd, inv[LH:], fil_fwd, z_prev, z, filt, feat, direction,
    )

    tok_coef, q_next = token_coef(sizes, seg_lengths, list_ids, proj, feat)

    grads, filter_part = pl.pallas_call(
        grad_kernel,
        grid_spec=pltpu.PrefetchScalarGridSpec(
            num_scalar_prefetch=1,
            grid=grid,
            in_specs=[
                const_spec((N2, N2)),
                const_spec((LH, N2)),
                const_spec((N2, LH)),
                const_spec((2 * rows, 1)),
                rows_spec(rows, width),
                rows_spec(rows, width),
                rows_spec(rows, width),
                rows_spec(1, width),
                stack_spec(3, rows, width),
                rows_spec(rows, width),
                rows_spec(rows, width),
                rows_spec(LH, width),
            ],
            out_specs=[stack_spec(3, rows, width), rows_spec(LH, width)],
            scratch_shapes=[
                pltpu.VMEM((2 * rows, width), BF16),
                pltpu.VMEM((rows, width), F32),
                pltpu.VMEM((N2, width), F32),
            ],
        ),
        out_shape=[
            jax.ShapeDtypeStruct((3, rows, chans), BF16),
            jax.ShapeDtypeStruct((LH, chans), BF16),
        ],
        name="grad",
    )(
        seg_lengths, fwd, inv[:LH], fil_fwd, tok_coef, upstream,
        up_next, q_next, direction, feat, mixed, z, filt,
    )

    half = chans // 2
    d_streams, d_taps, d_filter = pl.pallas_call(
        functools.partial(back_kernel, n_ctx, width),
        in_specs=[smem] + [vmem] * 5,
        out_specs=[vmem] * 3,
        out_shape=[
            jax.ShapeDtypeStruct((3, rows, chans), BF16),
            jax.ShapeDtypeStruct((3, 8, chans), F32),
            jax.ShapeDtypeStruct((shard_rows, chans), F32),
        ],
        scratch_shapes=[
            pltpu.VMEM((KF * rows, rows + 16), BF16),
            pltpu.VMEM((3, 16, chans), BF16),
            pltpu.VMEM((rows + 16, width), BF16),
            pltpu.VMEM((3, 8, chans), BF16),
            pltpu.VMEM((n_ctx, shard_rows, half), BF16),
            pltpu.VMEM((n_ctx, shard_rows, half), BF16),
            pltpu.VMEM((n_ctx, shard_rows, half), BF16),
            pltpu.VMEM((shard_rows, half), F32),
            pltpu.VMEM((3, 8, half), BF16),
            pltpu.VMEM((n_ctx, 3, 8, half), BF16),
            pltpu.VMEM((3, 8, half), BF16),
            pltpu.VMEM((3, 8, half), F32),
            dma((2,)),
            dma((2, 4)),
            dma((2, 4, n_ctx)),
            dma((2, 2)),
        ],
        compiler_params=pltpu.CompilerParams(collective_id=2, has_side_effects=True),
        name="back",
    )(seg_lengths, grads, streams, rim, feat_taps, filter_part.reshape(n_ctx, shard_rows, chans))
    return (d_streams, d_taps[:, :KF, :], d_filter)


def solution(mesh):
    placed = (
        P(None, ("groups", "ctx", "sub"), "fsdp"),
        P(None, None, "fsdp"),
        P("ctx", "fsdp"),
        P(("groups", "ctx", "sub"), "fsdp"),
        P("fsdp"),
        P("groups"),
        P("groups"),
    )
    sizes = (mesh.shape["ctx"], mesh.shape["fsdp"], mesh.shape["sub"])
    return jax.shard_map(
        functools.partial(local, sizes),
        mesh=mesh,
        in_specs=placed,
        out_specs=(
            P(None, ("groups", "ctx", "sub"), "fsdp"),
            P("groups", None, "fsdp"),
            P(("groups", "ctx"), "fsdp"),
        ),
        check_vma=False,
    )
```

```python
import functools

import jax
import jax.numpy as jnp
import numpy as np
from jax import lax
from jax.experimental import pallas as pl
from jax.experimental.pallas import tpu as pltpu
from jax.sharding import PartitionSpec as P

LH = 128
KF = 7
N2 = 2 * LH
F32 = jnp.float32
BF16 = jnp.bfloat16

_K, _N = np.meshgrid(np.arange(LH), np.arange(N2), indexing="ij")
_ANGLE = np.pi * (2 * _K + 1) * _N / N2
FWD = np.concatenate([np.cos(_ANGLE), -np.sin(_ANGLE)], axis=0).astype(np.float32)
INV = (FWD.T / LH).astype(np.float32)


def starts(lens_ref):
    offsets, off = [], jnp.int32(0)
    for s in range(lens_ref.shape[0]):
        offsets.append(off)
        off = off + lens_ref[s]
    return offsets


def segment_of(offsets, position):
    seg = jnp.where(offsets[0] <= position, 0, -1)
    for off in offsets[1:]:
        seg = seg + jnp.where(off <= position, 1, 0)
    return seg


def age_of(offsets, position):
    start = jnp.zeros(position.shape, jnp.int32)
    for off in offsets:
        start = jnp.where(off <= position, off, start)
    return position - start


def first_token(rows):
    return (lax.axis_index("ctx") * 2 + lax.axis_index("sub")) * rows


def down(rows):
    return lax.broadcasted_iota(jnp.int32, (rows, 1), 0)


def across(columns):
    return lax.broadcasted_iota(jnp.int32, (1, columns), 1)


def dot(a, b):
    return jnp.dot(a, b, preferred_element_type=F32)


MESH = pl.DeviceIdType.MESH


def place():
    group, ctx = lax.axis_index("groups"), lax.axis_index("ctx")
    fsdp, sub = lax.axis_index("fsdp"), lax.axis_index("sub")
    return group, ctx, fsdp, sub


def meet(n_ctx):
    group, ctx, fsdp, sub = place()
    line = ctx * 2 + sub
    barrier = pltpu.get_barrier_semaphore()
    left = (group, (line - 1) // 2, fsdp, 1 - sub)
    right = (group, (line + 1) // 2, fsdp, 1 - sub)

    @pl.when(line > 0)
    def _():
        pl.semaphore_signal(barrier, inc=1, device_id=left, device_id_type=MESH)

    @pl.when(line < 2 * n_ctx - 1)
    def _():
        pl.semaphore_signal(barrier, inc=1, device_id=right, device_id_type=MESH)

    pl.semaphore_signal(barrier, inc=1, device_id=(group, ctx, fsdp, 1 - sub), device_id_type=MESH)
    for r in range(1, n_ctx):
        pl.semaphore_signal(
            barrier, inc=1, device_id=(group, lax.rem(ctx + r, n_ctx), fsdp, sub),
            device_id_type=MESH,
        )
    ends = jnp.where(line > 0, 1, 0) + jnp.where(line < 2 * n_ctx - 1, 1, 0)
    pl.semaphore_wait(barrier, n_ctx + ends)
    return line > 0, line < 2 * n_ctx - 1, left, right


def send(src, dst, sems, device):
    return pltpu.make_async_remote_copy(
        src_ref=src, dst_ref=dst, send_sem=sems[0], recv_sem=sems[1], device_id=device,
        device_id_type=MESH,
    )


def feat_kernel(
    n_ctx, width, lens_ref, x_ref, taps_ref, fil_ref, up_ref, feat_ref, z_ref, prev_ref, next_ref,
    all_ref, shift_ref, rim_ref, ext_ref, rim_sem, z_sem, up_sem, fil_sem, swap_sem,
):
    group, ctx, fsdp, sub = place()
    rows, chans = x_ref.shape[1:]
    blocks = chans // width
    has_left, has_right, left, right = meet(n_ctx)
    partner = (group, ctx, fsdp, 1 - sub)

    def rim_copy():
        return send(
            x_ref.at[:, pl.ds(rows - 16, 16), :], rim_ref, (rim_sem.at[0], rim_sem.at[1]), right
        )

    def columns(b):
        return pl.ds(pl.multiple_of(b * width, width), width)

    def z_copy(b):
        return send(
            z_ref.at[:, columns(b)], prev_ref.at[:, columns(b)], (z_sem.at[0, b], z_sem.at[1, b]),
            right,
        )

    def up_copy():
        return send(up_ref, next_ref, (up_sem.at[0], up_sem.at[1]), left)

    def fil_copy(r):
        return send(
            fil_ref.at[sub], all_ref.at[ctx, sub], (fil_sem.at[0, r], fil_sem.at[1, r]),
            (group, lax.rem(ctx + r, n_ctx), fsdp, sub),
        )

    def swap_copy(r):
        held = lax.rem(ctx - r + n_ctx, n_ctx)
        return send(
            all_ref.at[held, sub], all_ref.at[held, sub], (swap_sem.at[0, r], swap_sem.at[1, r]),
            partner,
        )

    @pl.when(has_right)
    def _():
        rim_copy().start()

    for r in range(1, n_ctx):
        fil_copy(r).start()

    @pl.when(has_left)
    def _():
        up_copy().start()

    all_ref[ctx] = fil_ref[...]
    age = age_of(starts(lens_ref), first_token(rows) + down(rows))
    gap = across(rows + 16) - down(rows) - 16
    for j in range(KF):
        shift_ref[j * rows : (j + 1) * rows, :] = jnp.where(
            (gap == -j) & (age >= j), 1.0, 0.0
        ).astype(BF16)

    @pl.when(jnp.logical_not(has_left))
    def _():
        rim_ref[...] = jnp.zeros(rim_ref.shape, BF16)
        prev_ref[...] = jnp.zeros(prev_ref.shape, BF16)

    @pl.when(jnp.logical_not(has_right))
    def _():
        next_ref[...] = jnp.zeros(next_ref.shape, BF16)

    @pl.when(has_left)
    def _():
        rim_copy().wait_recv()

    def block(b, carry):
        cols = columns(b)
        feats = [None] * 3
        for i in (1, 2, 0):
            ext_ref[i, 0:16, :] = rim_ref[i, :, cols]
            ext_ref[i, 16:, :] = x_ref[i, :, cols]
            ext = ext_ref[i]
            total = jnp.zeros((rows, width), F32)
            for j in range(KF):
                total = total + taps_ref[i, j : j + 1, cols] * dot(
                    shift_ref[j * rows : (j + 1) * rows, :], ext
                )
            feats[i] = total.astype(BF16)
            feat_ref[i, :, cols] = feats[i]
            if i == 2:
                z_ref[:, cols] = (feats[1].astype(F32) * feats[2].astype(F32)).astype(BF16)

        @pl.when(has_right)
        def _():
            z_copy(b).start()

        return carry

    lax.fori_loop(0, blocks, block, 0)

    for r in range(1, n_ctx):
        fil_copy(r).wait()
        swap_copy(r).start()

    @pl.when(has_right)
    def _():
        rim_copy().wait_send()
        for b in range(blocks):
            z_copy(b).wait_send()
        up_copy().wait_recv()

    @pl.when(has_left)
    def _():
        for b in range(blocks):
            z_copy(b).wait_recv()
        up_copy().wait_send()

    for r in range(1, n_ctx):
        swap_copy(r).wait()


def mix_kernel(
    lens_ref, fwd_ref, inv_ref, fil_fwd_ref, prev_ref, z_ref, fil_ref, q_ref, dir_ref, w_ref, proj_ref, ext_ref,
):
    rows = z_ref.shape[0]
    offsets, base = starts(lens_ref), first_token(rows)
    colseg = segment_of(offsets, base - rows + across(2 * rows))
    rowseg = segment_of(offsets, base + down(rows))
    ext_ref[0:rows, :] = prev_ref[...]
    ext_ref[rows:, :] = z_ref[...]
    spec = dot(fil_fwd_ref[...], fil_ref[...])
    f_re, f_im = spec[:LH], spec[LH:]
    w_ref[...] = jnp.zeros(w_ref.shape, F32)

    def one(s, carry):
        fwd = jnp.where(colseg == s, fwd_ref[...], 0.0).astype(BF16)
        hat = dot(fwd, ext_ref[...])
        z_re, z_im = hat[:LH], hat[LH:]
        prod = jnp.concatenate(
            [(f_re * z_re - f_im * z_im).astype(BF16), (f_re * z_im + f_im * z_re).astype(BF16)],
            axis=0,
        )
        inv = jnp.where(rowseg == s, inv_ref[...], 0.0).astype(BF16)
        w_ref[...] += dot(inv, prod)
        return carry

    lowest, highest = segment_of(offsets, base), segment_of(offsets, base + rows - 1)
    lax.fori_loop(lowest, highest + 1, one, 0)
    weighted = q_ref[0].astype(F32) * w_ref[...] * dir_ref[...]
    part = weighted[:, 0:128]
    for b in range(1, weighted.shape[1] // 128):
        part = part + weighted[:, b * 128 : (b + 1) * 128]

    @pl.when(pl.program_id(0) == 0)
    def _():
        proj_ref[...] = jnp.zeros(proj_ref.shape, F32)

    proj_ref[...] += part


def grad_kernel(
    lens_ref, fwd_ref, inv_ref, fil_fwd_ref, tokcoef_ref, up_ref,
    up_next_ref, q_next_ref, dir_ref, feat_ref, w_ref, z_ref, fil_ref,
    da_ref, dfil_ref, ext_ref, dz_ref, corr_ref,
):
    rows = z_ref.shape[0]
    offsets, base = starts(lens_ref), first_token(rows)
    colseg = segment_of(offsets, base + across(2 * rows))
    rowseg = segment_of(offsets, base + down(rows))
    d_out = up_ref[...].astype(F32) + tokcoef_ref[0:rows, :] * dir_ref[...]
    da_ref[0] = (d_out * w_ref[...]).astype(BF16)
    ext_ref[0:rows, :] = (d_out * feat_ref[0].astype(F32)).astype(BF16)
    d_next = up_next_ref[...].astype(F32) + tokcoef_ref[rows:, :] * dir_ref[...]
    ext_ref[rows:, :] = (d_next * q_next_ref[...].astype(F32)).astype(BF16)
    spec = dot(fil_fwd_ref[...], fil_ref[...])
    f_re, f_im = spec[:LH], spec[LH:]
    dz_ref[...] = jnp.zeros(dz_ref.shape, F32)
    corr_ref[...] = jnp.zeros(corr_ref.shape, F32)

    def one(s, carry):
        fwd = jnp.where(colseg == s, fwd_ref[...], 0.0).astype(BF16)
        hat = dot(fwd, ext_ref[...])
        d_re, d_im = hat[:LH], hat[LH:]
        prod = jnp.concatenate(
            [(f_re * d_re + f_im * d_im).astype(BF16), (f_re * d_im - f_im * d_re).astype(BF16)],
            axis=0,
        )
        inv = jnp.where(rowseg == s, inv_ref[...], 0.0).astype(BF16)
        dz_ref[...] += dot(inv, prod)
        zhat = dot(fwd[:, :rows], z_ref[...])
        z_re, z_im = zhat[:LH], zhat[LH:]
        corr_ref[:LH] += z_re * d_re + z_im * d_im
        corr_ref[LH:] += z_re * d_im - z_im * d_re
        return carry

    lowest, highest = segment_of(offsets, base), segment_of(offsets, base + rows - 1)
    lax.fori_loop(lowest, highest + 1, one, 0)
    d_prod = dz_ref[...]
    da_ref[1] = (d_prod * feat_ref[2].astype(F32)).astype(BF16)
    da_ref[2] = (d_prod * feat_ref[1].astype(F32)).astype(BF16)
    dfil_ref[...] = dot(inv_ref[...].astype(BF16), corr_ref[...].astype(BF16)).astype(BF16)


def back_kernel(
    n_ctx, width, lens_ref, da_ref, x_ref, taps_ref, dfil_ref, dx_ref, dtaps_ref, out_ref,
    shift_ref, halo_ref, ext_ref, tap_ref, fil_a, fil_b, fil_c, fil_sum, tap_a, tap_b, tap_c, tap_sum,
    halo_sem, a_sem, b_sem, c_sem,
):
    group, ctx, fsdp, sub = place()
    rows, chans = x_ref.shape[1:]
    half = chans // 2
    has_left, has_right, left, right = meet(n_ctx)
    partner = (group, ctx, fsdp, 1 - sub)
    kept = pl.ds(pl.multiple_of(sub * half, half), half)
    given = pl.ds(pl.multiple_of((1 - sub) * half, half), half)

    def halo_copy():
        return send(
            da_ref.at[:, pl.ds(0, 16), :], halo_ref, (halo_sem.at[0], halo_sem.at[1]), left
        )

    first = [send(dfil_ref.at[:, :, given], fil_a, (a_sem.at[0, 0], a_sem.at[1, 0]), partner)]
    for i in range(3):
        first.append(
            send(
                tap_ref.at[i, :, given], tap_a.at[i], (a_sem.at[0, 1 + i], a_sem.at[1, 1 + i]),
                partner,
            )
        )

    def second(c, r):
        sems = (b_sem.at[0, c, r], b_sem.at[1, c, r])
        owner = lax.rem(ctx + r, n_ctx)
        target = (group, owner, fsdp, sub)
        if c == 0:
            return send(fil_c.at[owner], fil_b.at[r], sems, target)
        return send(tap_c.at[c - 1], tap_b.at[r, c - 1], sems, target)

    last = [
        send(fil_sum, out_ref.at[:, kept], (c_sem.at[0, 0], c_sem.at[1, 0]), partner),
        send(tap_sum, dtaps_ref.at[:, :, kept], (c_sem.at[0, 1], c_sem.at[1, 1]), partner),
    ]

    @pl.when(has_left)
    def _():
        halo_copy().start()

    first[0].start()

    @pl.when(jnp.logical_not(has_right))
    def _():
        halo_ref[...] = jnp.zeros(halo_ref.shape, BF16)

    age = age_of(starts(lens_ref), first_token(rows) + across(rows + 16))
    gap = across(rows + 16) - down(rows)
    for j in range(KF):
        shift_ref[j * rows : (j + 1) * rows, :] = jnp.where(
            (gap == j) & (age >= j), 1.0, 0.0
        ).astype(BF16)

    def stream(i):
        def block(b, carry):
            cols = pl.ds(pl.multiple_of(b * width, width), width)
            ext_ref[0:rows, :] = da_ref[i, :, cols]
            ext_ref[rows:, :] = halo_ref[i, :, cols]
            ext = ext_ref[...]
            own = x_ref[i, :, cols].astype(F32)
            total = jnp.zeros((rows, width), F32)
            sums = []
            for j in range(KF):
                moved = dot(shift_ref[j * rows : (j + 1) * rows, :], ext)
                total = total + taps_ref[i, j : j + 1, cols] * moved
                sums.append(jnp.sum(own * moved, axis=0, keepdims=True))
            sums.append(jnp.zeros((1, width), F32))
            tap_ref[i, :, cols] = jnp.concatenate(sums, axis=0).astype(BF16)
            dx_ref[i, :, cols] = total.astype(BF16)
            return carry

        lax.fori_loop(0, chans // width, block, 0)

    def relay(c):
        first[c].wait()
        if c == 0:
            fil_c[...] = (dfil_ref[:, :, kept].astype(F32) + fil_a[...].astype(F32)).astype(BF16)
        else:
            i = c - 1
            tap_c[i] = (tap_ref[i, :, kept].astype(F32) + tap_a[i].astype(F32)).astype(BF16)
        for r in range(1, n_ctx):
            second(c, r).start()

    relay(0)

    @pl.when(has_right)
    def _():
        halo_copy().wait_recv()

    stream(0)
    first[1].start()
    stream(1)
    first[2].start()
    relay(1)
    stream(2)
    first[3].start()
    relay(2)
    relay(3)
    for r in range(1, n_ctx):
        second(0, r).wait()
    total = fil_c[ctx].astype(F32)
    for r in range(1, n_ctx):
        total = total + fil_b[r].astype(F32)
    fil_sum[...] = total
    out_ref[:, kept] = total
    last[0].start()
    for c in range(1, 4):
        for r in range(1, n_ctx):
            second(c, r).wait()
    tap_b[0] = tap_c[...]

    def add(d, running):
        return running + tap_b[lax.rem(ctx - d + n_ctx, n_ctx)].astype(F32)

    taps_total = lax.fori_loop(0, n_ctx, add, jnp.zeros(tap_sum.shape, F32))
    tap_sum[...] = taps_total
    dtaps_ref[:, :, kept] = taps_total
    last[1].start()
    last[0].wait()
    last[1].wait()

    @pl.when(has_left)
    def _():
        halo_copy().wait_send()


def const_spec(shape):
    return pl.BlockSpec(shape, lambda b, *_: (0,) * len(shape))


def rows_spec(rows, width):
    return pl.BlockSpec((rows, width), lambda b, *_: (0, b))


def stack_spec(count, rows, width):
    return pl.BlockSpec((count, rows, width), lambda b, *_: (0, 0, b))


def total_kernel(
    sizes, lens_ref, ids_ref, proj_ref, feat_ref, out_ref, next_ref, part_ref, slots, send_sem,
    recv_sem, q_sem,
):
    n_ctx, n_fsdp, n_sub = sizes
    count = n_ctx * n_fsdp * n_sub
    me = (lax.axis_index("ctx") * n_fsdp + lax.axis_index("fsdp")) * n_sub + lax.axis_index("sub")
    group = lax.axis_index("groups")

    def where(r):
        peer = lax.rem(me + r, count)
        return (
            group,
            peer // (n_fsdp * n_sub),
            lax.rem(peer // n_sub, n_fsdp),
            lax.rem(peer, n_sub),
        )

    barrier = pltpu.get_barrier_semaphore()

    def greet(r, carry):
        pl.semaphore_signal(
            barrier, inc=1, device_id=where(r), device_id_type=pl.DeviceIdType.MESH
        )
        return carry

    lax.fori_loop(1, count, greet, 0)
    segs, rows = part_ref.shape[0], proj_ref.shape[0]
    offsets, base = starts(lens_ref), first_token(rows)
    rowseg = segment_of(offsets, base + down(rows))
    for s in range(segs):
        part_ref[s : s + 1, :] = jnp.sum(
            jnp.where(rowseg == s, proj_ref[...], 0.0), axis=0, keepdims=True
        )
    pl.semaphore_wait(barrier, count - 1)

    def copy(r):
        return pltpu.make_async_remote_copy(
            src_ref=part_ref,
            dst_ref=slots.at[r],
            send_sem=send_sem.at[r],
            recv_sem=recv_sem.at[r],
            device_id=where(r),
            device_id_type=pl.DeviceIdType.MESH,
        )

    def begin(r, carry):
        copy(r).start()
        return carry

    def end(r, carry):
        copy(r).wait()
        return carry

    _, ctx, fsdp, sub = place()
    line = ctx * 2 + sub
    q_copy = send(
        feat_ref.at[0], next_ref, (q_sem.at[0], q_sem.at[1]), (group, (line - 1) // 2, fsdp, 1 - sub)
    )
    lax.fori_loop(1, count, begin, 0)

    @pl.when(line > 0)
    def _():
        q_copy.start()

    @pl.when(line == 2 * n_ctx - 1)
    def _():
        next_ref[...] = jnp.zeros(next_ref.shape, BF16)

    lax.fori_loop(1, count, end, 0)
    slots[0] = part_ref[...]

    def add(i, total):
        return total + slots[lax.rem(me - i + count, count)]

    summed = lax.fori_loop(0, count, add, jnp.zeros(part_ref.shape, F32))
    ids, id_row = jnp.zeros((segs, 1), jnp.int32), jnp.zeros((1, segs), jnp.int32)
    lengths = jnp.zeros((segs, 1), jnp.int32)
    for s in range(segs):
        ids = jnp.where(down(segs) == s, ids_ref[s], ids)
        id_row = jnp.where(across(segs) == s, ids_ref[s], id_row)
        lengths = jnp.where(down(segs) == s, lens_ref[s], lengths)
    lengths = lengths.astype(F32)
    scores = jnp.sum(summed, axis=1, keepdims=True) / lengths
    same = down(segs) == across(segs)
    score_row = jnp.sum(jnp.where(same, scores, 0.0), axis=0, keepdims=True)
    mates = jnp.where(ids == id_row, 1.0, 0.0)
    means = jnp.sum(mates * score_row, axis=1, keepdims=True) / jnp.sum(
        mates, axis=1, keepdims=True
    )
    coef = (scores - means) / lengths
    coef_row = jnp.sum(jnp.where(same, coef, 0.0), axis=0, keepdims=True)
    hot = segment_of(offsets, base + down(2 * rows)) == across(segs)
    out_ref[...] = jnp.sum(jnp.where(hot, coef_row, 0.0), axis=1, keepdims=True)

    @pl.when(line > 0)
    def _():
        q_copy.wait_send()

    @pl.when(line < 2 * n_ctx - 1)
    def _():
        q_copy.wait_recv()


def token_coef(sizes, seg_lengths, list_ids, proj, feat):
    count = sizes[0] * sizes[1] * sizes[2]
    segs = seg_lengths.shape[0]
    rows, chans = feat.shape[1:]
    smem = pl.BlockSpec(memory_space=pltpu.SMEM)
    vmem = pl.BlockSpec(memory_space=pltpu.VMEM)
    return pl.pallas_call(
        functools.partial(total_kernel, sizes),
        out_shape=[
            jax.ShapeDtypeStruct((2 * rows, 1), F32), jax.ShapeDtypeStruct((rows, chans), BF16)
        ],
        in_specs=[smem, smem, vmem, pl.BlockSpec(memory_space=pl.ANY)],
        out_specs=[vmem, vmem],
        scratch_shapes=[
            pltpu.VMEM((segs, 128), F32),
            pltpu.VMEM((count, segs, 128), F32),
            pltpu.SemaphoreType.DMA((count,)),
            pltpu.SemaphoreType.DMA((count,)),
            pltpu.SemaphoreType.DMA((2,)),
        ],
        compiler_params=pltpu.CompilerParams(collective_id=0, has_side_effects=True),
        name="token_coef",
    )(seg_lengths, list_ids, proj, feat)


def local(sizes, streams, feat_taps, long_filter, upstream, score_dir, seg_lengths, list_ids):
    rows, chans = streams.shape[1:]
    width = min(512, chans)
    grid = (chans // width,)

    n_ctx = sizes[0]
    shard_rows = long_filter.shape[0]
    vmem = pl.BlockSpec(memory_space=pltpu.VMEM)
    smem = pl.BlockSpec(memory_space=pltpu.SMEM)
    dma = pltpu.SemaphoreType.DMA

    fwd = jnp.asarray(FWD)
    inv = jnp.asarray(INV)
    fil_fwd = jnp.asarray(FWD[:, :LH], BF16)

    blocks = chans // width
    feat, z, z_prev, up_next, filt = pl.pallas_call(
        functools.partial(feat_kernel, n_ctx, width),
        in_specs=[smem, vmem, vmem, vmem, pl.BlockSpec(memory_space=pl.ANY)],
        out_specs=[vmem] * 5,
        out_shape=[
            jax.ShapeDtypeStruct((3, rows, chans), BF16),
            jax.ShapeDtypeStruct((rows, chans), BF16),
            jax.ShapeDtypeStruct((rows, chans), BF16),
            jax.ShapeDtypeStruct((rows, chans), BF16),
            jax.ShapeDtypeStruct((n_ctx, 2, shard_rows // 2, chans), BF16),
        ],
        scratch_shapes=[
            pltpu.VMEM((KF * rows, rows + 16), BF16),
            pltpu.VMEM((3, 16, chans), BF16),
            pltpu.VMEM((3, rows + 16, width), BF16),
            dma((2,)),
            dma((2, blocks)),
            dma((2,)),
            dma((2, n_ctx)),
            dma((2, n_ctx)),
        ],
        compiler_params=pltpu.CompilerParams(collective_id=1, has_side_effects=True),
        name="feat",
    )(seg_lengths, streams, feat_taps, long_filter.reshape(2, shard_rows // 2, chans), upstream)
    filt = filt.reshape(LH, chans)
    direction = score_dir[None, :]

    mixed, proj = pl.pallas_call(
        mix_kernel,
        grid_spec=pltpu.PrefetchScalarGridSpec(
            num_scalar_prefetch=1,
            grid=grid,
            in_specs=[
                const_spec((N2, N2)),
                const_spec((LH, N2)),
                const_spec((N2, LH)),
                rows_spec(rows, width),
                rows_spec(rows, width),
                rows_spec(LH, width),
                stack_spec(1, rows, width),
                rows_spec(1, width),
            ],
            out_specs=[rows_spec(rows, width), const_spec((rows, 128))],
            scratch_shapes=[pltpu.VMEM((2 * rows, width), BF16)],
        ),
        out_shape=[
            jax.ShapeDtypeStruct((rows, chans), F32),
            jax.ShapeDtypeStruct((rows, 128), F32),
        ],
        name="mix",
    )(
        seg_lengths, fwd, inv[LH:], fil_fwd, z_prev, z, filt, feat, direction,
    )

    tok_coef, q_next = token_coef(sizes, seg_lengths, list_ids, proj, feat)

    grads, filter_part = pl.pallas_call(
        grad_kernel,
        grid_spec=pltpu.PrefetchScalarGridSpec(
            num_scalar_prefetch=1,
            grid=grid,
            in_specs=[
                const_spec((N2, N2)),
                const_spec((LH, N2)),
                const_spec((N2, LH)),
                const_spec((2 * rows, 1)),
                rows_spec(rows, width),
                rows_spec(rows, width),
                rows_spec(rows, width),
                rows_spec(1, width),
                stack_spec(3, rows, width),
                rows_spec(rows, width),
                rows_spec(rows, width),
                rows_spec(LH, width),
            ],
            out_specs=[stack_spec(3, rows, width), rows_spec(LH, width)],
            scratch_shapes=[
                pltpu.VMEM((2 * rows, width), BF16),
                pltpu.VMEM((rows, width), F32),
                pltpu.VMEM((N2, width), F32),
            ],
        ),
        out_shape=[
            jax.ShapeDtypeStruct((3, rows, chans), BF16),
            jax.ShapeDtypeStruct((LH, chans), BF16),
        ],
        name="grad",
    )(
        seg_lengths, fwd, inv[:LH], fil_fwd, tok_coef, upstream,
        up_next, q_next, direction, feat, mixed, z, filt,
    )

    half = chans // 2
    d_streams, d_taps, d_filter = pl.pallas_call(
        functools.partial(back_kernel, n_ctx, width),
        in_specs=[smem] + [vmem] * 4,
        out_specs=[vmem] * 3,
        out_shape=[
            jax.ShapeDtypeStruct((3, rows, chans), BF16),
            jax.ShapeDtypeStruct((3, 8, chans), F32),
            jax.ShapeDtypeStruct((shard_rows, chans), F32),
        ],
        scratch_shapes=[
            pltpu.VMEM((KF * rows, rows + 16), BF16),
            pltpu.VMEM((3, 16, chans), BF16),
            pltpu.VMEM((rows + 16, width), BF16),
            pltpu.VMEM((3, 8, chans), BF16),
            pltpu.VMEM((n_ctx, shard_rows, half), BF16),
            pltpu.VMEM((n_ctx, shard_rows, half), BF16),
            pltpu.VMEM((n_ctx, shard_rows, half), BF16),
            pltpu.VMEM((shard_rows, half), F32),
            pltpu.VMEM((3, 8, half), BF16),
            pltpu.VMEM((n_ctx, 3, 8, half), BF16),
            pltpu.VMEM((3, 8, half), BF16),
            pltpu.VMEM((3, 8, half), F32),
            dma((2,)),
            dma((2, 4)),
            dma((2, 4, n_ctx)),
            dma((2, 2)),
        ],
        compiler_params=pltpu.CompilerParams(collective_id=2, has_side_effects=True),
        name="back",
    )(seg_lengths, grads, streams, feat_taps, filter_part.reshape(n_ctx, shard_rows, chans))
    return (d_streams, d_taps[:, :KF, :], d_filter)


def solution(mesh):
    placed = (
        P(None, ("groups", "ctx", "sub"), "fsdp"),
        P(None, None, "fsdp"),
        P("ctx", "fsdp"),
        P(("groups", "ctx", "sub"), "fsdp"),
        P("fsdp"),
        P("groups"),
        P("groups"),
    )
    sizes = (mesh.shape["ctx"], mesh.shape["fsdp"], mesh.shape["sub"])
    return jax.shard_map(
        functools.partial(local, sizes),
        mesh=mesh,
        in_specs=placed,
        out_specs=(
            P(None, ("groups", "ctx", "sub"), "fsdp"),
            P("groups", None, "fsdp"),
            P(("groups", "ctx"), "fsdp"),
        ),
        check_vma=False,
    )
```
